768 devices in a mesh: chan: 48 (over y_lo, z), space: 16 (over x, y_hi, core).
Axes of the slice: x: 4, y: 8 (y_hi: 2, y_lo: 4; y = y_hi * 4 + y_lo), z: 12, core: 2. Of those that a mesh axis runs over, the one named last changes fastest.
Arguments:
- floor_tokens: int32 [128, 128], P('space'), may hold values from 0 to 255
- token_table: bfloat16 [256, 1536], P(None, 'chan'), may hold values from -6 to 6
- depth_kernel: bfloat16 [7, 7, 1536], P(None, None, 'chan'), may hold values from -2 to 2
- norm_gain: float32 [1536], replicated, may hold values from 0.5 to 1.5
- layer_scale: float32 [1536], replicated, may hold values from 0.5 to 2
- w_in: bfloat16 [1536, 6144], P(None, 'chan'), may hold values from -0.375 to 0.375
- w_out: bfloat16 [6144, 1536], P('chan'), may hold values from -0.1875 to 0.1875
- grad_out: bfloat16 [128, 128, 1536], P('space', None, 'chan'), may hold values from -6 to 6
Outputs:
- block_out: bfloat16 [128, 128, 1536], P('space', None, 'chan')
- grad_embedded: bfloat16 [128, 128, 1536], P('space', None, 'chan')
The draws below stay inside these ranges and needn't reach their ends.
Inputs may be any that keep to these rules, and one draw needn't show every extreme that they name: `floor_tokens`: token ids of the floor cells.
All inputs are finite; a program needn't handle non-finite values.
Results may differ from the reference program's by a relative error of at most 0.0067.
Values may be sent and summed in bfloat16 or wider, within the bound.
No kernel may reach another device: no remote copies, remote signals or barrier semaphores. Data moves between devices by JAX's collectives and lax.ppermute only.
A program may use at most 128 MiB of HBM per device.

```python
import math
import jax
import jax.numpy as jnp
import numpy as np
from jax import lax

D = 1536
HID = 6144
VOCAB = 256
KS = 7
COLS = 128
ROWS = 128


def place_ends(drawn, key, smallest, high):
    longest = drawn.shape.index(max(drawn.shape))
    spots = []
    for shift in (0, 1):
        where = [jax.random.randint(jax.random.fold_in(key, axis), (), 0, length) for axis, length in enumerate(drawn.shape)]
        where[longest] = (where[longest] + shift) % drawn.shape[longest]
        spots.append(tuple(where))
    return drawn.at[spots[0]].set(smallest).at[spots[1]].set(high)


def with_spikes(drawn, key, source, target, parts, factor):
    def block_of(dim):
        return (jnp.arange(drawn.shape[dim]) // (drawn.shape[dim] // parts)).reshape((-1,) + (1,) * (drawn.ndim - 1 - dim))

    one_side = jax.random.permutation(key, parts)[block_of(target)]
    other_side = (block_of(target) + parts // 2) % parts
    return jnp.where((block_of(source) == one_side) | (block_of(source) == other_side), factor * drawn, drawn)


def block_levels(rng, dims, split, low, high):
    factor_of, own = 1.0, jax.random.fold_in(rng, 6)
    for position, parts in split:
        draws = jnp.exp(jax.random.uniform(jax.random.fold_in(own, position), (parts,), jnp.float32, low / len(split), high / len(split)))
        factor_of = factor_of * jnp.repeat(draws, dims[position] // parts).reshape([-1 if axis == position else 1 for axis in range(len(dims))])
    return factor_of


def rank_bounds(number_of, slope):
    portions = [(1 << 20) // math.isqrt(rank ** slope) + 1 for rank in range(1, number_of + 1)]
    width = 1 + sum(portions) // (1 << 30)
    return np.cumsum(np.array([max(1, weight // width) for weight in portions]))


def skewed_ids(stream_key, dims, number_of, slope):
    listing = rank_bounds(number_of, slope)
    pick = jax.random.randint(jax.random.fold_in(stream_key, 1), dims, 0, int(listing[number_of - 1]))
    rank = jnp.searchsorted(jnp.asarray(listing, jnp.int32), pick, side="right")
    return jax.random.permutation(jax.random.fold_in(stream_key, 2), number_of)[rank].astype(jnp.int32)


def noise(rng, dims, deviation, most, pieces=(), kind=jnp.bfloat16):
    loudness = block_levels(rng, dims, pieces, -0.22, 0.18) if pieces else 1.0
    drawn = jax.random.normal(rng, dims, jnp.float32) * deviation * loudness
    return jnp.minimum(jnp.maximum(drawn, -most), most).astype(kind)


def bell_draw_with(own_key, dims, scale, bound, split, heavy, held_as=jnp.bfloat16):
    drawn = scale * jax.random.normal(own_key, dims, jnp.float32)
    if split:
        drawn = drawn * block_levels(own_key, dims, split, -0.22, 0.18)
    return jnp.clip(with_spikes(drawn, jax.random.fold_in(own_key, 3), *heavy), -bound, bound).astype(held_as)


def setup_inputs(seed: int = 0) -> dict:
    splits = jax.random.split(jax.random.key(seed), 9)
    floor_tokens = place_ends(skewed_ids(splits[0], (ROWS, COLS), VOCAB, 2), jax.random.fold_in(splits[0], 3), 0, VOCAB - 1).astype(jnp.int32)
    token_table = noise(splits[1], (VOCAB, D), 1.0, 6.0, ((1, 48),))
    depth_kernel = noise(splits[2], (KS, KS, D), 0.15, 2.0, ((2, 48),))
    norm_gain = jnp.clip(1.0 + 0.1 * jax.random.normal(splits[3], (D,), jnp.float32), 0.5, 1.5)
    layer_scale = jnp.clip(jnp.exp(jax.random.uniform(splits[4], (D,), jnp.float32, math.log(0.5), math.log(2.0))), 0.5, 2.0)
    w_in = bell_draw_with(splits[5], (D, HID), D ** -0.5, 0.375, ((1, 48),), (1, 0, 48, 3.25))
    w_out = bell_draw_with(splits[6], (HID, D), HID ** -0.5, 0.1875, ((0, 48),), (0, 1, 48, 3.25))
    grad_out = noise(splits[7], (ROWS, COLS, D), 1.0, 6.0, ((0, 16), (2, 48)))
    return dict(floor_tokens=floor_tokens, token_table=token_table, depth_kernel=depth_kernel, norm_gain=norm_gain, layer_scale=layer_scale, w_in=w_in, w_out=w_out, grad_out=grad_out)


def forward_conv(padded, depth_kernel, rows, cols):
    total = jnp.zeros((rows, cols, padded.shape[2]), jnp.float32)
    for row_off in range(KS):
        for col_off in range(KS):
            window = padded[row_off:row_off + rows, col_off:col_off + cols].astype(jnp.float32)
            total = total + window * depth_kernel[row_off, col_off].astype(jnp.float32)
    return total

def backward_conv(padded, depth_kernel, rows, cols):
    total = jnp.zeros((rows, cols, padded.shape[2]), jnp.float32)
    for row_off in range(KS):
        for col_off in range(KS):
            start_row = KS - 1 - row_off
            start_col = KS - 1 - col_off
            window = padded[start_row:start_row + rows, start_col:start_col + cols].astype(jnp.float32)
            total = total + window * depth_kernel[row_off, col_off].astype(jnp.float32)
    return total

def gelu_tanh(value):
    return jax.nn.gelu(value, approximate=True)

def reference(floor_tokens, token_table, depth_kernel, norm_gain, layer_scale, w_in, w_out, grad_out):
    rows, cols = floor_tokens.shape
    embedded = jnp.take(token_table, floor_tokens, axis=0)
    padded = jnp.pad(embedded, ((3, 3), (3, 3), (0, 0)))
    conv = forward_conv(padded, depth_kernel, rows, cols).astype(jnp.bfloat16)
    flat = conv.reshape(rows * cols, D).astype(jnp.float32)
    row_mean = lax.optimization_barrier(jnp.mean(flat, axis=-1, keepdims=True))
    centered = flat - row_mean
    inv_std = jax.lax.rsqrt(lax.optimization_barrier(jnp.mean(centered * centered, axis=-1, keepdims=True)) + 1e-06)
    normed = centered * inv_std
    scaled = (normed * norm_gain).astype(jnp.bfloat16)
    pre = jnp.dot(scaled, w_in, preferred_element_type=jnp.float32)
    act = gelu_tanh(pre).astype(jnp.bfloat16)
    mix = jnp.dot(act, w_out, preferred_element_type=jnp.float32)
    base = embedded.reshape(rows * cols, D).astype(jnp.float32)
    block_out = (base + layer_scale * mix).astype(jnp.bfloat16).reshape(rows, cols, D)
    grad_flat = grad_out.reshape(rows * cols, D)
    grad_mix = (layer_scale * grad_flat.astype(jnp.float32)).astype(jnp.bfloat16)
    grad_act = jnp.dot(grad_mix, w_out.T, preferred_element_type=jnp.float32)
    grad_pre = jax.vjp(gelu_tanh, pre)[1](grad_act)[0].astype(jnp.bfloat16)
    grad_norm = jnp.dot(grad_pre, w_in.T, preferred_element_type=jnp.float32)
    scaled_grad = grad_norm * norm_gain
    grad_conv = inv_std * (scaled_grad - lax.optimization_barrier(jnp.mean(scaled_grad, axis=-1, keepdims=True)) - normed * lax.optimization_barrier(jnp.mean(scaled_grad * normed, axis=-1, keepdims=True)))
    grad_conv = grad_conv.astype(jnp.bfloat16).reshape(rows, cols, D)
    grad_padded = jnp.pad(grad_conv, ((3, 3), (3, 3), (0, 0)))
    through = backward_conv(grad_padded, depth_kernel, rows, cols)
    grad_embedded = (grad_out.astype(jnp.float32) + through).astype(jnp.bfloat16)
    return (block_out, grad_embedded)
```

```python
import jax
import jax.numpy as jnp
from jax import lax
from jax.sharding import Mesh, PartitionSpec as P

AXES = ("y", "z", "x", "h", "c")
CHAN = ("y", "z")
SPACE = ("x", "h", "c")


def halo(block, width):
    count = lax.axis_size(SPACE)
    forward = [(i, i + 1) for i in range(count - 1)]
    backward = [(j, i) for i, j in forward]
    low = lax.ppermute(block[block.shape[0] - width :], SPACE, forward)
    high = lax.ppermute(block[:width], SPACE, backward)
    return jnp.concatenate([low, block, high], axis=0)


def conv49(framed, kernel, rows, flip):
    cols = framed.shape[2]
    padded = jnp.pad(framed, ((0, 0), (0, 0), (3, 3)))
    total = jnp.zeros((rows, framed.shape[1], cols), jnp.float32)
    for a in range(7):
        for b in range(7):
            i, j = (6 - a, 6 - b) if flip else (a, b)
            window = padded[i : i + rows, :, j : j + cols].astype(jnp.float32)
            total = total + window * kernel[a, b].astype(jnp.float32)[None, :, None]
    return total


def gelu_tanh(value):
    return jax.nn.gelu(value, approximate=True)


def spread(strip):
    ny, nz = lax.axis_size("y"), lax.axis_size("z")
    rows, chans, cols = strip.shape
    part = rows // ny
    blocks = strip.reshape(ny, 1, part, chans, cols)
    blocks = jnp.broadcast_to(blocks, (ny, nz, part, chans, cols)).reshape(ny * nz, part, chans, cols)
    got = lax.all_to_all(blocks, CHAN, 0, 0, tiled=True)
    return got.transpose(0, 2, 1, 3).reshape(ny * nz * chans, part * cols)


def collect(total, part):
    ny, nz = lax.axis_size("y"), lax.axis_size("z")
    chans, cols = total.shape[0] // (ny * nz), total.shape[1] // part
    blocks = total.astype(jnp.bfloat16).reshape(ny * nz, chans, part, cols).transpose(0, 2, 1, 3)
    got = lax.all_to_all(blocks, CHAN, 0, 0, tiled=True)
    got = got.reshape(ny, nz, part, chans, cols).astype(jnp.float32)
    return jnp.sum(got, axis=1).reshape(ny * part, chans, cols)


def on_device(
    floor_tokens, token_table, depth_kernel, norm_gain, layer_scale, w_in, w_out, grad_out
):
    rows, cols = floor_tokens.shape
    chans = depth_kernel.shape[2]
    part = rows // lax.axis_size("y")
    offset = lax.axis_index(CHAN) * chans
    grad_local = grad_out.transpose(0, 2, 1)
    grad = spread(grad_local).astype(jnp.float32)
    x_local = jnp.take(token_table, floor_tokens, axis=0).transpose(0, 2, 1)
    conv_local = conv49(halo(x_local, 3), depth_kernel, rows, False).astype(jnp.bfloat16)
    w_in = lax.all_gather(w_in, "y", axis=1, tiled=True)
    w_out = lax.all_gather(w_out, "y", axis=0, tiled=True)
    conv = spread(conv_local).astype(jnp.float32)

    gain = norm_gain[:, None]
    mean = jnp.mean(conv, axis=0, keepdims=True)
    centered = conv - mean
    inv_std = lax.rsqrt(jnp.mean(centered * centered, axis=0, keepdims=True) + 1e-06)
    normed = centered * inv_std
    scaled = (normed * gain).astype(jnp.bfloat16)
    pre = lax.dot_general(w_in, scaled, (((0,), (0,)), ((), ())), preferred_element_type=jnp.float32)
    grad_mix = (layer_scale[:, None] * grad).astype(jnp.bfloat16)
    grad_act = jnp.dot(w_out, grad_mix, preferred_element_type=jnp.float32)
    act, vjp = jax.vjp(gelu_tanh, pre)
    mix = lax.dot_general(
        w_out, act.astype(jnp.bfloat16), (((0,), (0,)), ((), ())), preferred_element_type=jnp.float32
    )
    mix = collect(mix, part)
    grad_pre = vjp(grad_act)[0].astype(jnp.bfloat16)
    scaled_grad = jnp.dot(w_in, grad_pre, preferred_element_type=jnp.float32) * gain
    conv_part = inv_std * (
        scaled_grad
        - jnp.mean(scaled_grad, axis=0, keepdims=True)
        - normed * jnp.mean(scaled_grad * normed, axis=0, keepdims=True)
    )
    grad_conv = collect(conv_part, part).astype(jnp.bfloat16)

    scale_local = lax.dynamic_slice_in_dim(layer_scale, offset, chans, 0)[None, :, None]
    block_out = (x_local.astype(jnp.float32) + scale_local * mix).astype(jnp.bfloat16)
    through = conv49(halo(grad_conv, 3), depth_kernel, rows, True)
    grad_embedded = (grad_local.astype(jnp.float32) + through).astype(jnp.bfloat16)
    return block_out.transpose(0, 2, 1), grad_embedded.transpose(0, 2, 1)


def solution(mesh):
    chan, space = mesh.shape["chan"], mesh.shape["space"]
    grid = Mesh(mesh.devices.reshape(4, chan // 4, space // 4, 2, 2), AXES)
    placed = (
        P(SPACE, None),
        P(None, CHAN),
        P(None, None, CHAN),
        P(),
        P(),
        P(None, CHAN),
        P(CHAN, None),
        P(SPACE, None, CHAN),
    )
    return jax.shard_map(
        on_device,
        mesh=grid,
        in_specs=placed,
        out_specs=(P(SPACE, None, CHAN), P(SPACE, None, CHAN)),
        check_vma=False,
    )
```

```python
import functools
import math

import jax
import jax.numpy as jnp
from jax import lax
from jax.experimental import pallas as pl
from jax.experimental.pallas import tpu as pltpu
from jax.sharding import Mesh, PartitionSpec as P

AXES = ("y", "z", "x", "h", "c")
CHAN = ("y", "z")
SPACE = ("x", "h", "c")
BF16, F32 = jnp.bfloat16, jnp.float32
VMEM = pl.BlockSpec(memory_space=pltpu.VMEM)
ANY = pl.BlockSpec(memory_space=pl.ANY)
ROOT = math.sqrt(2.0 / math.pi)


def edges(low_side, high_side):
    count = lax.axis_size(SPACE)
    forward = [(i, i + 1) for i in range(count - 1)]
    backward = [(j, i) for i, j in forward]
    return lax.ppermute(high_side, SPACE, forward), lax.ppermute(low_side, SPACE, backward)


def conv_rows(framed, taps_ref, flip, emit):
    rows = len(framed) - 6
    chans, cols = framed[0].shape
    lane = lax.broadcasted_iota(jnp.int32, (chans, cols), 1)
    totals = [jnp.zeros((chans, cols), F32) for _ in range(rows)]
    for b in range(7):
        step = (6 - b if flip else b) - 3
        taps = [
            jnp.broadcast_to(taps_ref[:, a * 7 + b : a * 7 + b + 1].astype(F32), (chans, cols))
            for a in range(7)
        ]
        inside = (lane + step >= 0) & (lane + step < cols)
        for i, tile in enumerate(framed):
            if step:
                tile = jnp.where(inside, pltpu.roll(tile, (-step) % cols, 1), 0.0)
            for a in range(7):
                r = i - (6 - a if flip else a)
                if 0 <= r < rows:
                    totals[r] = totals[r] + tile * taps[a]
    for r in range(rows):
        emit(r, totals[r])


def first_kernel(copies, tok_ref, low_ref, high_ref, table_ref, taps_ref, scale_ref, grad_ref, x_ref, send_ref):
    rows, cols = tok_ref.shape
    chans, vocab = table_ref.shape
    ident = lax.broadcasted_iota(jnp.int32, (vocab, cols), 0) + 1
    lines = [low_ref[i : i + 1] for i in range(3)]
    lines += [tok_ref[i : i + 1] + 1 for i in range(rows)]
    lines += [high_ref[i : i + 1] for i in range(3)]
    framed = []
    for line in lines:
        hot = (ident == line).astype(F32).astype(BF16)
        framed.append(jnp.dot(table_ref[...], hot, preferred_element_type=F32))
    for r in range(rows):
        x_ref[r] = framed[r + 3].astype(BF16)

    def targets(r):
        return [(r // 2) * 2 * copies + 2 * k + r % 2 for k in range(copies)]

    scale = jnp.broadcast_to(scale_ref[...], (chans, cols))
    for r in range(rows):
        mixed = (grad_ref[r].astype(F32) * scale).astype(BF16)
        for d in targets(r):
            send_ref[d, 1] = mixed

    def emit(r, total):
        total = total.astype(BF16)
        for d in targets(r):
            send_ref[d, 0] = total

    conv_rows(framed, taps_ref, False, emit)


def middle_kernel(
    own_ref, oth_ref, gain_ref, w0_ref, w1_ref, w2_ref, w3_ref,
    keep_ref, sib_ref,
    win, wout, scaled, gmix, normed, grads, act, gpre, sem,
):
    blocks, _, chans, cols = own_ref.shape
    width = blocks * chans
    hid = w0_ref.shape[1]
    pieces = [(ref.at[0], ref.at[1]) for ref in (w0_ref, w1_ref, w2_ref, w3_ref)]
    copies = []
    for i, (a, b) in enumerate(pieces):
        spot = pl.ds(i * hid, hid)
        copies.append(pltpu.make_async_copy(a, win.at[spot], sem.at[2 * i]))
        copies.append(pltpu.make_async_copy(b, wout.at[spot], sem.at[2 * i + 1]))
    for copy in copies:
        copy.start()

    def cell(s, t):
        return jnp.concatenate([own_ref[s, t], oth_ref[s, t]], axis=1)

    zero = jnp.zeros((chans, 2 * cols), F32)
    total = lax.fori_loop(0, blocks, lambda s, acc: acc + cell(s, 0).astype(F32), zero, unroll=8)
    mean = jnp.sum(total, axis=0, keepdims=True) * (1.0 / width)

    def square(s, acc):
        diff = cell(s, 0).astype(F32) - mean
        return acc + diff * diff

    total = lax.fori_loop(0, blocks, square, zero, unroll=8)
    inv_std = lax.rsqrt(jnp.sum(total, axis=0, keepdims=True) * (1.0 / width) + 1e-06)

    def norm(s, carry):
        spot = pl.ds(pl.multiple_of(s * chans, chans), chans)
        value = (cell(s, 0).astype(F32) - mean) * inv_std
        gain = gain_ref[spot, :]
        normed[spot, :] = value
        scaled[spot, :] = (value * jnp.concatenate([gain, gain], axis=1)).astype(BF16)
        gmix[spot, :] = cell(s, 1)
        return carry

    lax.fori_loop(0, blocks, norm, 0, unroll=4)
    for copy in copies:
        copy.wait()

    for i in range(len(pieces)):
        spot = pl.ds(i * hid, hid)
        pre = jnp.dot(win[spot, :], scaled[...], preferred_element_type=F32)
        gact = jnp.dot(wout[spot, :], gmix[...], preferred_element_type=F32)
        cube = pre * pre
        tanh = jnp.tanh(ROOT * (pre + 0.044715 * (cube * pre)))
        half = 0.5 * (1.0 + tanh)
        act[spot, :] = (pre * half).astype(BF16)
        slope = half + (0.5 * pre) * (1.0 - tanh * tanh) * (ROOT * (1.0 + 0.134145 * cube))
        gpre[spot, :] = (gact * slope).astype(BF16)

    group = 256
    per = group // chans
    sums = [jnp.zeros((1, 2 * cols), F32), jnp.zeros((1, 2 * cols), F32)]
    turned = (((0,), (0,)), ((), ()))
    for j in range(width // group):
        spot = pl.ds(j * group, group)
        gain = gain_ref[spot, :]
        part = lax.dot_general(win[:, spot], gpre[...], turned, preferred_element_type=F32)
        part = part * jnp.concatenate([gain, gain], axis=1)
        grads[spot, :] = part
        sums[0] = sums[0] + jnp.sum(part, axis=0, keepdims=True)
        sums[1] = sums[1] + jnp.sum(part * normed[spot, :], axis=0, keepdims=True)
        mix = lax.dot_general(wout[:, spot], act[...], turned, preferred_element_type=F32)
        for q in range(per):
            piece = mix[q * chans : (q + 1) * chans]
            keep_ref[j * per + q, 0] = piece[:, :cols]
            sib_ref[j * per + q, 0] = piece[:, cols:].astype(BF16)
    first, second = sums[0] * (1.0 / width), sums[1] * (1.0 / width)

    def finish(s, carry):
        spot = pl.ds(pl.multiple_of(s * chans, chans), chans)
        piece = inv_std * (grads[spot, :] - first - normed[spot, :] * second)
        keep_ref[s, 1] = piece[:, :cols]
        sib_ref[s, 1] = piece[:, cols:].astype(BF16)
        return carry

    lax.fori_loop(0, blocks, finish, 0, unroll=4)


def sum_kernel(copies, got_ref, x_ref, scale_ref, out_ref, gconv_ref, low_ref, high_ref):
    rows, chans, cols = x_ref.shape
    scale = jnp.broadcast_to(scale_ref[...], (chans, cols))
    for r in range(rows):
        base = (r // 2) * 2 * copies + r % 2
        mix = got_ref[base, 0].astype(F32)
        conv = got_ref[base, 1].astype(F32)
        for k in range(1, copies):
            mix = mix + got_ref[base + 2 * k, 0].astype(F32)
            conv = conv + got_ref[base + 2 * k, 1].astype(F32)
        out_ref[r] = (x_ref[r].astype(F32) + scale * mix).astype(BF16)
        conv = conv.astype(BF16)
        gconv_ref[r] = conv
        if r < 3:
            low_ref[r] = conv
        if r >= rows - 3:
            high_ref[r - rows + 3] = conv


def last_kernel(gconv_ref, low_ref, high_ref, taps_ref, grad_ref, out_ref):
    rows = gconv_ref.shape[0]
    framed = [low_ref[i].astype(F32) for i in range(3)]
    framed += [gconv_ref[i].astype(F32) for i in range(rows)]
    framed += [high_ref[i].astype(F32) for i in range(3)]

    def emit(r, total):
        out_ref[r] = (grad_ref[r].astype(F32) + total).astype(BF16)

    conv_rows(framed, taps_ref, True, emit)


def call(body, outs, args, specs=None, scratch=(), flops=1 << 20, limit=32 << 20):
    outs = [jax.ShapeDtypeStruct(s, d) for s, d in outs]
    return pl.pallas_call(
        body,
        out_shape=outs,
        in_specs=specs or [VMEM] * len(args),
        out_specs=[VMEM] * len(outs),
        scratch_shapes=list(scratch),
        compiler_params=pltpu.CompilerParams(vmem_limit_bytes=limit),
        cost_estimate=pl.CostEstimate(flops=flops, bytes_accessed=4 << 20, transcendentals=0),
    )(*args)


def pair_weights(w_in, w_out):
    both = jnp.stack([w_in.T, w_out])
    nz, nh, ny = lax.axis_size("z"), lax.axis_size("h"), lax.axis_size("y")
    pairs = []
    for z in range(nz):
        for c in range(2):
            other = (z, c) if z % 2 == c else (z ^ 1, 1 - c)
            pairs.append((other[0] * 2 + other[1], z * 2 + c))
    return lax.ppermute(both, ("z", "c"), pairs)


def ring_weights(both):
    nh, ny = lax.axis_size("h"), lax.axis_size("y")
    ring = [y * nh + h for h in range(nh) for y in range(ny)]
    count = len(ring)

    def from_steps(steps):
        pairs = [
            (ring[(i + steps[c]) % count] * 2 + c, ring[i] * 2 + c) for i in range(count) for c in range(2)
        ]
        return lax.ppermute(both, ("y", "h", "c"), pairs)

    return both, from_steps((2, -2)), from_steps((1, 1)), from_steps((-1, -1))


def on_device(
    floor_tokens, token_table, depth_kernel, norm_gain, layer_scale, w_in, w_out, grad_out
):
    rows, cols = floor_tokens.shape
    chans = depth_kernel.shape[2]
    width = norm_gain.shape[0]
    blocks = width // chans
    copies = lax.axis_size("z") // 2
    hid = w_out.shape[0] * lax.axis_size("y")
    swap = [(0, 1), (1, 0)]

    both = pair_weights(w_in, w_out)
    low, high = edges(floor_tokens[:3] + 1, floor_tokens[rows - 3 :] + 1)
    taps = depth_kernel.reshape(49, chans).T
    scale = lax.dynamic_slice_in_dim(layer_scale, lax.axis_index(CHAN) * chans, chans, 0)[:, None]
    gain = jnp.broadcast_to(norm_gain[:, None], (width, cols))
    grad_local = grad_out.transpose(0, 2, 1)

    tile = (rows, chans, cols)
    packed = (blocks, 2, chans, cols)
    x_local, send = call(
        functools.partial(first_kernel, copies),
        [(tile, BF16), (packed, BF16)],
        (floor_tokens, low, high, token_table.T, taps, scale, grad_local),
    )
    send, both = lax.optimization_barrier((send, both))
    weights = ring_weights(both)
    own = lax.all_to_all(send, CHAN, 0, 0, tiled=True)
    oth = lax.ppermute(own, "c", swap)
    keep, sib = call(
        middle_kernel,
        [(packed, F32), (packed, BF16)],
        (own, oth, gain, *weights),
        [VMEM] * 3 + [ANY] * 4,
        [
            pltpu.VMEM((hid, width), BF16),
            pltpu.VMEM((hid, width), BF16),
            pltpu.VMEM((width, 2 * cols), BF16),
            pltpu.VMEM((width, 2 * cols), BF16),
            pltpu.VMEM((width, 2 * cols), F32),
            pltpu.VMEM((width, 2 * cols), F32),
            pltpu.VMEM((hid, 2 * cols), BF16),
            pltpu.VMEM((hid, 2 * cols), BF16),
            pltpu.SemaphoreType.DMA((8,)),
        ],
        flops=8 * hid * width * 2 * cols,
        limit=40 << 20,
    )
    part = (keep + lax.ppermute(sib, "c", swap).astype(F32)).astype(BF16)
    got = lax.all_to_all(part, CHAN, 0, 0, tiled=True)
    edge = (3, chans, cols)
    block_out, gconv, low_side, high_side = call(
        functools.partial(sum_kernel, copies),
        [(tile, BF16), (tile, BF16), (edge, BF16), (edge, BF16)],
        (got, x_local, scale),
    )
    low, high = edges(low_side, high_side)
    (grad_embedded,) = call(last_kernel, [(tile, BF16)], (gconv, low, high, taps, grad_local))
    return block_out.transpose(0, 2, 1), grad_embedded.transpose(0, 2, 1)


def solution(mesh):
    chan, space = mesh.shape["chan"], mesh.shape["space"]
    grid = Mesh(mesh.devices.reshape(4, chan // 4, space // 4, 2, 2), AXES)
    placed = (
        P(SPACE, None),
        P(None, CHAN),
        P(None, None, CHAN),
        P(),
        P(),
        P(None, CHAN),
        P(CHAN, None),
        P(SPACE, None, CHAN),
    )
    return jax.shard_map(
        on_device,
        mesh=grid,
        in_specs=placed,
        out_specs=(P(SPACE, None, CHAN), P(SPACE, None, CHAN)),
        check_vma=False,
    )
```

```python
import functools
import itertools
import math

import jax
import jax.numpy as jnp
from jax import lax
from jax.experimental import pallas as pl
from jax.experimental.pallas import tpu as pltpu
from jax.sharding import Mesh, PartitionSpec as P

AXES = ("y", "z", "x", "h", "c")
CHAN = ("y", "z")
SPACE = ("x", "h", "c")
BF16, F32 = jnp.bfloat16, jnp.float32
VMEM = pl.BlockSpec(memory_space=pltpu.VMEM)
ANY = pl.BlockSpec(memory_space=pl.ANY)
ROOT = math.sqrt(2.0 / math.pi)


def edges(low_side, high_side):
    count = lax.axis_size(SPACE)
    forward = [(i, i + 1) for i in range(count - 1)]
    backward = [(j, i) for i, j in forward]
    return lax.ppermute(high_side, SPACE, forward), lax.ppermute(low_side, SPACE, backward)


def conv_rows(framed, taps_ref, flip, emit):
    rows = len(framed) - 6
    chans, cols = framed[0].shape
    lane = lax.broadcasted_iota(jnp.int32, (chans, cols), 1)
    totals = [jnp.zeros((chans, cols), F32) for _ in range(rows)]
    for b in range(7):
        step = (6 - b if flip else b) - 3
        taps = [
            jnp.broadcast_to(taps_ref[:, a * 7 + b : a * 7 + b + 1].astype(F32), (chans, cols))
            for a in range(7)
        ]
        inside = (lane + step >= 0) & (lane + step < cols)
        for i, tile in enumerate(framed):
            if step:
                tile = jnp.where(inside, pltpu.roll(tile, (-step) % cols, 1), 0.0)
            for a in range(7):
                r = i - (6 - a if flip else a)
                if 0 <= r < rows:
                    totals[r] = totals[r] + tile * taps[a]
    for r in range(rows):
        emit(r, totals[r])


def first_kernel(copies, tok_ref, low_ref, high_ref, table_ref, taps_ref, scale_ref, grad_ref, x_ref, send_ref):
    rows, cols = tok_ref.shape
    chans, vocab = table_ref.shape
    ident = lax.broadcasted_iota(jnp.int32, (vocab, cols), 0) + 1
    lines = [low_ref[i : i + 1] for i in range(3)]
    lines += [tok_ref[i : i + 1] + 1 for i in range(rows)]
    lines += [high_ref[i : i + 1] for i in range(3)]
    framed = []
    for line in lines:
        hot = (ident == line).astype(F32).astype(BF16)
        framed.append(jnp.dot(table_ref[...], hot, preferred_element_type=F32))
    for r in range(rows):
        x_ref[r] = framed[r + 3].astype(BF16)

    def targets(r):
        return [(r // 2) * 2 * copies + 2 * k + r % 2 for k in range(copies)]

    scale = jnp.broadcast_to(scale_ref[...], (chans, cols))
    for r in range(rows):
        mixed = (grad_ref[r].astype(F32) * scale).astype(BF16)
        for d in targets(r):
            send_ref[d, 1] = mixed

    def emit(r, total):
        total = total.astype(BF16)
        for d in targets(r):
            send_ref[d, 0] = total

    conv_rows(framed, taps_ref, False, emit)


def middle_kernel(
    own_ref, oth_ref, gain_ref, i0_ref, i1_ref, i2_ref, i3_ref, o0_ref, o1_ref, o2_ref, o3_ref,
    keep_ref, sib_ref,
    win, wout, scaled, gmix, normed, grads, act, gpre, sem,
):
    blocks, _, chans, cols = own_ref.shape
    width = blocks * chans
    hid = o0_ref.shape[0]
    pieces = [(i0_ref, o0_ref), (i1_ref, o1_ref), (i2_ref, o2_ref), (i3_ref, o3_ref)]
    copies = []
    for i, (a, b) in enumerate(pieces):
        spot = pl.ds(i * hid, hid)
        copies.append(pltpu.make_async_copy(a, win.at[:, spot], sem.at[2 * i]))
        copies.append(pltpu.make_async_copy(b, wout.at[spot], sem.at[2 * i + 1]))
    for copy in copies:
        copy.start()

    def cell(s, t):
        return jnp.concatenate([own_ref[s, t], oth_ref[s, t]], axis=1)

    zero = jnp.zeros((chans, 2 * cols), F32)
    total = lax.fori_loop(0, blocks, lambda s, acc: acc + cell(s, 0).astype(F32), zero, unroll=8)
    mean = jnp.sum(total, axis=0, keepdims=True) * (1.0 / width)

    def square(s, acc):
        diff = cell(s, 0).astype(F32) - mean
        return acc + diff * diff

    total = lax.fori_loop(0, blocks, square, zero, unroll=8)
    inv_std = lax.rsqrt(jnp.sum(total, axis=0, keepdims=True) * (1.0 / width) + 1e-06)

    def norm(s, carry):
        spot = pl.ds(pl.multiple_of(s * chans, chans), chans)
        value = (cell(s, 0).astype(F32) - mean) * inv_std
        gain = gain_ref[spot, :]
        normed[spot, :] = value
        scaled[spot, :] = (value * jnp.concatenate([gain, gain], axis=1)).astype(BF16)
        gmix[spot, :] = cell(s, 1)
        return carry

    lax.fori_loop(0, blocks, norm, 0, unroll=4)
    for copy in copies:
        copy.wait()

    turned = (((0,), (0,)), ((), ()))
    for i in range(len(pieces)):
        spot = pl.ds(i * hid, hid)
        pre = lax.dot_general(win[:, spot], scaled[...], turned, preferred_element_type=F32)
        gact = jnp.dot(wout[spot, :], gmix[...], preferred_element_type=F32)
        cube = pre * pre
        tanh = jnp.tanh(ROOT * (pre + 0.044715 * (cube * pre)))
        half = 0.5 * (1.0 + tanh)
        act[spot, :] = (pre * half).astype(BF16)
        slope = half + (0.5 * pre) * (1.0 - tanh * tanh) * (ROOT * (1.0 + 0.134145 * cube))
        gpre[spot, :] = (gact * slope).astype(BF16)

    group = 256
    per = group // chans
    sums = [jnp.zeros((1, 2 * cols), F32), jnp.zeros((1, 2 * cols), F32)]
    for j in range(width // group):
        spot = pl.ds(j * group, group)
        gain = gain_ref[spot, :]
        part = jnp.dot(win[spot, :], gpre[...], preferred_element_type=F32)
        part = part * jnp.concatenate([gain, gain], axis=1)
        grads[spot, :] = part
        sums[0] = sums[0] + jnp.sum(part, axis=0, keepdims=True)
        sums[1] = sums[1] + jnp.sum(part * normed[spot, :], axis=0, keepdims=True)
        mix = lax.dot_general(wout[:, spot], act[...], turned, preferred_element_type=F32)
        for q in range(per):
            piece = mix[q * chans : (q + 1) * chans]
            keep_ref[j * per + q, 0] = piece[:, :cols]
            sib_ref[j * per + q, 0] = piece[:, cols:].astype(BF16)
    first, second = sums[0] * (1.0 / width), sums[1] * (1.0 / width)

    def finish(s, carry):
        spot = pl.ds(pl.multiple_of(s * chans, chans), chans)
        piece = inv_std * (grads[spot, :] - first - normed[spot, :] * second)
        keep_ref[s, 1] = piece[:, :cols]
        sib_ref[s, 1] = piece[:, cols:].astype(BF16)
        return carry

    lax.fori_loop(0, blocks, finish, 0, unroll=4)


def sum_kernel(copies, got_ref, x_ref, scale_ref, out_ref, gconv_ref, low_ref, high_ref):
    rows, chans, cols = x_ref.shape
    scale = jnp.broadcast_to(scale_ref[...], (chans, cols))
    for r in range(rows):
        base = (r // 2) * 2 * copies + r % 2
        mix = got_ref[base, 0].astype(F32)
        conv = got_ref[base, 1].astype(F32)
        for k in range(1, copies):
            mix = mix + got_ref[base + 2 * k, 0].astype(F32)
            conv = conv + got_ref[base + 2 * k, 1].astype(F32)
        out_ref[r] = (x_ref[r].astype(F32) + scale * mix).astype(BF16)
        conv = conv.astype(BF16)
        gconv_ref[r] = conv
        if r < 3:
            low_ref[r] = conv
        if r >= rows - 3:
            high_ref[r - rows + 3] = conv


def last_kernel(gconv_ref, low_ref, high_ref, taps_ref, grad_ref, out_ref):
    rows = gconv_ref.shape[0]
    framed = [low_ref[i].astype(F32) for i in range(3)]
    framed += [gconv_ref[i].astype(F32) for i in range(rows)]
    framed += [high_ref[i].astype(F32) for i in range(3)]

    def emit(r, total):
        out_ref[r] = (grad_ref[r].astype(F32) + total).astype(BF16)

    conv_rows(framed, taps_ref, True, emit)


def call(body, outs, args, specs=None, scratch=(), flops=1 << 20, limit=32 << 20):
    outs = [jax.ShapeDtypeStruct(s, d) for s, d in outs]
    return pl.pallas_call(
        body,
        out_shape=outs,
        in_specs=specs or [VMEM] * len(args),
        out_specs=[VMEM] * len(outs),
        scratch_shapes=list(scratch),
        compiler_params=pltpu.CompilerParams(vmem_limit_bytes=limit),
        cost_estimate=pl.CostEstimate(flops=flops, bytes_accessed=4 << 20, transcendentals=0),
    )(*args)


def shifted(shard):
    ny, nz, nx, nh, nc = (lax.axis_size(a) for a in AXES)
    count = ny * nh

    def place(y, z, x, h, c):
        return (((y * nz + z) * nx + x) * nh + h) * nc + c

    pairs = []
    for y, z, x, h, c in itertools.product(*[range(n) for n in (ny, nz, nx, nh, nc)]):
        turn = x % ny
        if 2 * turn == ny and c:
            turn = -turn
        spot = (h * ny + y + turn) % count
        other = (z, c) if z % 2 == c else (z ^ 1, 1 - c)
        pairs.append((place(spot % ny, other[0], x, spot // ny, other[1]), place(y, z, x, h, c)))
    return lax.ppermute(shard, AXES, pairs)


def gathered(shard):
    nx = lax.axis_size("x")
    others = [lax.ppermute(shard, "x", [((i + k) % nx, i) for i in range(nx)]) for k in (2, 1, 3)]
    return [shard, *others]


def on_device(
    floor_tokens, token_table, depth_kernel, norm_gain, layer_scale, w_in, w_out, grad_out
):
    rows, cols = floor_tokens.shape
    chans = depth_kernel.shape[2]
    width = norm_gain.shape[0]
    blocks = width // chans
    copies = lax.axis_size("z") // 2
    hid = w_out.shape[0] * lax.axis_size("y")
    swap = [(0, 1), (1, 0)]

    w_in = shifted(w_in)
    low, high = edges(floor_tokens[:3] + 1, floor_tokens[rows - 3 :] + 1)
    taps = depth_kernel.reshape(49, chans).T
    scale = lax.dynamic_slice_in_dim(layer_scale, lax.axis_index(CHAN) * chans, chans, 0)[:, None]
    gain = jnp.broadcast_to(norm_gain[:, None], (width, cols))
    grad_local = grad_out.transpose(0, 2, 1)

    tile = (rows, chans, cols)
    packed = (blocks, 2, chans, cols)
    x_local, send = call(
        functools.partial(first_kernel, copies),
        [(tile, BF16), (packed, BF16)],
        (floor_tokens, low, high, token_table.T, taps, scale, grad_local),
    )
    send, w_in = lax.optimization_barrier((send, w_in))
    w_out = shifted(w_out)
    weights = gathered(w_in)
    w_out, weights[1] = lax.optimization_barrier((w_out, weights[1]))
    weights = weights + gathered(w_out)
    own = lax.all_to_all(send, CHAN, 0, 0, tiled=True)
    own, *weights = lax.optimization_barrier((own, *weights))
    oth = lax.ppermute(own, "c", swap)
    keep, sib = call(
        middle_kernel,
        [(packed, F32), (packed, BF16)],
        (own, oth, gain, *weights),
        [VMEM] * 3 + [ANY] * 8,
        [
            pltpu.VMEM((width, hid), BF16),
            pltpu.VMEM((hid, width), BF16),
            pltpu.VMEM((width, 2 * cols), BF16),
            pltpu.VMEM((width, 2 * cols), BF16),
            pltpu.VMEM((width, 2 * cols), F32),
            pltpu.VMEM((width, 2 * cols), F32),
            pltpu.VMEM((hid, 2 * cols), BF16),
            pltpu.VMEM((hid, 2 * cols), BF16),
            pltpu.SemaphoreType.DMA((8,)),
        ],
        flops=8 * hid * width * 2 * cols,
        limit=40 << 20,
    )
    part = (keep + lax.ppermute(sib, "c", swap).astype(F32)).astype(BF16)
    got = lax.all_to_all(part, CHAN, 0, 0, tiled=True)
    edge = (3, chans, cols)
    block_out, gconv, low_side, high_side = call(
        functools.partial(sum_kernel, copies),
        [(tile, BF16), (tile, BF16), (edge, BF16), (edge, BF16)],
        (got, x_local, scale),
    )
    low, high = edges(low_side, high_side)
    (grad_embedded,) = call(last_kernel, [(tile, BF16)], (gconv, low, high, taps, grad_local))
    return block_out.transpose(0, 2, 1), grad_embedded.transpose(0, 2, 1)


def solution(mesh):
    chan, space = mesh.shape["chan"], mesh.shape["space"]
    grid = Mesh(mesh.devices.reshape(4, chan // 4, space // 4, 2, 2), AXES)
    placed = (
        P(SPACE, None),
        P(None, CHAN),
        P(None, None, CHAN),
        P(),
        P(),
        P(None, CHAN),
        P(CHAN, None),
        P(SPACE, None, CHAN),
    )
    return jax.shard_map(
        on_device,
        mesh=grid,
        in_specs=placed,
        out_specs=(P(SPACE, None, CHAN), P(SPACE, None, CHAN)),
        check_vma=False,
    )
```

```python
import functools
import itertools
import math

import jax
import jax.numpy as jnp
from jax import lax
from jax.experimental import pallas as pl
from jax.experimental.pallas import tpu as pltpu
from jax.sharding import Mesh, PartitionSpec as P

AXES = ("y", "z", "x", "h", "c")
CHAN = ("y", "z")
SPACE = ("x", "h", "c")
BF16, F32 = jnp.bfloat16, jnp.float32
VMEM = pl.BlockSpec(memory_space=pltpu.VMEM)
ANY = pl.BlockSpec(memory_space=pl.ANY)
ROOT = math.sqrt(2.0 / math.pi)


def edges(low_side, high_side):
    count = lax.axis_size(SPACE)
    forward = [(i, i + 1) for i in range(count - 1)]
    backward = [(j, i) for i, j in forward]
    return lax.ppermute(high_side, SPACE, forward), lax.ppermute(low_side, SPACE, backward)


def conv_rows(framed, taps_ref, flip, emit):
    rows = len(framed) - 6
    chans, cols = framed[0].shape
    lane = lax.broadcasted_iota(jnp.int32, (chans, cols), 1)
    totals = [jnp.zeros((chans, cols), F32) for _ in range(rows)]
    for b in range(7):
        step = (6 - b if flip else b) - 3
        taps = [
            jnp.broadcast_to(taps_ref[:, a * 7 + b : a * 7 + b + 1].astype(F32), (chans, cols))
            for a in range(7)
        ]
        inside = (lane + step >= 0) & (lane + step < cols)
        for i, tile in enumerate(framed):
            if step:
                tile = jnp.where(inside, pltpu.roll(tile, (-step) % cols, 1), 0.0)
            for a in range(7):
                r = i - (6 - a if flip else a)
                if 0 <= r < rows:
                    totals[r] = totals[r] + tile * taps[a]
    for r in range(rows):
        emit(r, totals[r])


def first_kernel(copies, tok_ref, low_ref, high_ref, table_ref, taps_ref, scale_ref, grad_ref, x_ref, send_ref):
    rows, cols = tok_ref.shape
    chans, vocab = table_ref.shape
    ident = lax.broadcasted_iota(jnp.int32, (vocab, cols), 0) + 1
    lines = [low_ref[i : i + 1] for i in range(3)]
    lines += [tok_ref[i : i + 1] + 1 for i in range(rows)]
    lines += [high_ref[i : i + 1] for i in range(3)]
    framed = []
    for line in lines:
        hot = (ident == line).astype(F32).astype(BF16)
        framed.append(jnp.dot(table_ref[...], hot, preferred_element_type=F32))
    for r in range(rows):
        x_ref[r] = framed[r + 3].astype(BF16)

    def targets(r):
        return [(r // 2) * 2 * copies + 2 * k + r % 2 for k in range(copies)]

    scale = jnp.broadcast_to(scale_ref[...], (chans, cols))
    for r in range(rows):
        mixed = (grad_ref[r].astype(F32) * scale).astype(BF16)
        for d in targets(r):
            send_ref[d, 1] = mixed

    def emit(r, total):
        total = total.astype(BF16)
        for d in targets(r):
            send_ref[d, 0] = total

    conv_rows(framed, taps_ref, False, emit)


def middle_kernel(
    own_ref, oth_ref, gain_ref, i0_ref, i1_ref, i2_ref, i3_ref, o0_ref, o1_ref, o2_ref, o3_ref,
    keep_ref, sib_ref,
    win, wout, scaled, gmix, normed, grads, act, gpre, sem,
):
    blocks, _, chans, cols = own_ref.shape
    width = blocks * chans
    hid = o0_ref.shape[0]
    pieces = [(i0_ref, o0_ref), (i1_ref, o1_ref), (i2_ref, o2_ref), (i3_ref, o3_ref)]
    copies = []
    for i, (a, b) in enumerate(pieces):
        spot = pl.ds(i * hid, hid)
        copies.append(pltpu.make_async_copy(a, win.at[:, spot], sem.at[2 * i]))
        copies.append(pltpu.make_async_copy(b, wout.at[spot], sem.at[2 * i + 1]))
    for copy in copies:
        copy.start()

    def cell(s, t):
        return jnp.concatenate([own_ref[s, t], oth_ref[s, t]], axis=1)

    zero = jnp.zeros((chans, 2 * cols), F32)
    total = lax.fori_loop(0, blocks, lambda s, acc: acc + cell(s, 0).astype(F32), zero, unroll=8)
    mean = jnp.sum(total, axis=0, keepdims=True) * (1.0 / width)

    def square(s, acc):
        diff = cell(s, 0).astype(F32) - mean
        return acc + diff * diff

    total = lax.fori_loop(0, blocks, square, zero, unroll=8)
    inv_std = lax.rsqrt(jnp.sum(total, axis=0, keepdims=True) * (1.0 / width) + 1e-06)

    def norm(s, carry):
        spot = pl.ds(pl.multiple_of(s * chans, chans), chans)
        value = (cell(s, 0).astype(F32) - mean) * inv_std
        gain = gain_ref[spot, :]
        normed[spot, :] = value
        scaled[spot, :] = (value * jnp.concatenate([gain, gain], axis=1)).astype(BF16)
        gmix[spot, :] = cell(s, 1)
        return carry

    lax.fori_loop(0, blocks, norm, 0, unroll=4)
    for copy in copies:
        copy.wait()

    turned = (((0,), (0,)), ((), ()))
    for i in range(len(pieces)):
        spot = pl.ds(i * hid, hid)
        pre = lax.dot_general(win[:, spot], scaled[...], turned, preferred_element_type=F32)
        gact = jnp.dot(wout[spot, :], gmix[...], preferred_element_type=F32)
        cube = pre * pre
        tanh = jnp.tanh(ROOT * (pre + 0.044715 * (cube * pre)))
        half = 0.5 * (1.0 + tanh)
        act[spot, :] = (pre * half).astype(BF16)
        slope = half + (0.5 * pre) * (1.0 - tanh * tanh) * (ROOT * (1.0 + 0.134145 * cube))
        gpre[spot, :] = (gact * slope).astype(BF16)

    group = 256
    per = group // chans
    sums = [jnp.zeros((1, 2 * cols), F32), jnp.zeros((1, 2 * cols), F32)]
    for j in range(width // group):
        spot = pl.ds(j * group, group)
        gain = gain_ref[spot, :]
        part = jnp.dot(win[spot, :], gpre[...], preferred_element_type=F32)
        part = part * jnp.concatenate([gain, gain], axis=1)
        grads[spot, :] = part
        sums[0] = sums[0] + jnp.sum(part, axis=0, keepdims=True)
        sums[1] = sums[1] + jnp.sum(part * normed[spot, :], axis=0, keepdims=True)
        mix = lax.dot_general(wout[:, spot], act[...], turned, preferred_element_type=F32)
        for q in range(per):
            piece = mix[q * chans : (q + 1) * chans]
            keep_ref[j * per + q, 0] = piece[:, :cols]
            sib_ref[j * per + q, 0] = piece[:, cols:].astype(BF16)
    first, second = sums[0] * (1.0 / width), sums[1] * (1.0 / width)

    def finish(s, carry):
        spot = pl.ds(pl.multiple_of(s * chans, chans), chans)
        piece = inv_std * (grads[spot, :] - first - normed[spot, :] * second)
        keep_ref[s, 1] = piece[:, :cols]
        sib_ref[s, 1] = piece[:, cols:].astype(BF16)
        return carry

    lax.fori_loop(0, blocks, finish, 0, unroll=4)


def sum_kernel(copies, got_ref, x_ref, scale_ref, out_ref, gconv_ref, low_ref, high_ref):
    rows, chans, cols = x_ref.shape
    scale = jnp.broadcast_to(scale_ref[...], (chans, cols))
    for r in range(rows):
        base = (r // 2) * 2 * copies + r % 2
        mix = got_ref[base, 0].astype(F32)
        conv = got_ref[base, 1].astype(F32)
        for k in range(1, copies):
            mix = mix + got_ref[base + 2 * k, 0].astype(F32)
            conv = conv + got_ref[base + 2 * k, 1].astype(F32)
        out_ref[r] = (x_ref[r].astype(F32) + scale * mix).astype(BF16)
        conv = conv.astype(BF16)
        gconv_ref[r] = conv
        if r < 3:
            low_ref[r] = conv
        if r >= rows - 3:
            high_ref[r - rows + 3] = conv


def last_kernel(gconv_ref, low_ref, high_ref, taps_ref, grad_ref, out_ref):
    rows = gconv_ref.shape[0]
    framed = [low_ref[i].astype(F32) for i in range(3)]
    framed += [gconv_ref[i].astype(F32) for i in range(rows)]
    framed += [high_ref[i].astype(F32) for i in range(3)]

    def emit(r, total):
        out_ref[r] = (grad_ref[r].astype(F32) + total).astype(BF16)

    conv_rows(framed, taps_ref, True, emit)


def call(body, outs, args, specs=None, scratch=(), flops=1 << 20, limit=32 << 20):
    outs = [jax.ShapeDtypeStruct(s, d) for s, d in outs]
    return pl.pallas_call(
        body,
        out_shape=outs,
        in_specs=specs or [VMEM] * len(args),
        out_specs=[VMEM] * len(outs),
        scratch_shapes=list(scratch),
        compiler_params=pltpu.CompilerParams(vmem_limit_bytes=limit),
        cost_estimate=pl.CostEstimate(flops=flops, bytes_accessed=4 << 20, transcendentals=0),
    )(*args)


def shifted(shard):
    ny, nz, nx, nh, nc = (lax.axis_size(a) for a in AXES)
    count = ny * nh

    def place(y, z, x, h, c):
        return (((y * nz + z) * nx + x) * nh + h) * nc + c

    pairs = []
    for y, z, x, h, c in itertools.product(*[range(n) for n in (ny, nz, nx, nh, nc)]):
        turn = x % ny
        if 2 * turn > ny or (2 * turn == ny and c):
            turn -= ny
        spot = (h * ny + y + turn) % count
        other = (z, c) if z % 2 == c else (z ^ 1, 1 - c)
        pairs.append((place(spot % ny, other[0], x, spot // ny, other[1]), place(y, z, x, h, c)))
    return lax.ppermute(shard, AXES, pairs)


def gathered(shard):
    nx = lax.axis_size("x")
    others = [lax.ppermute(shard, "x", [((i + k) % nx, i) for i in range(nx)]) for k in (2, 1, 3)]
    return [shard, *others]


def on_device(
    floor_tokens, token_table, depth_kernel, norm_gain, layer_scale, w_in, w_out, grad_out
):
    rows, cols = floor_tokens.shape
    chans = depth_kernel.shape[2]
    width = norm_gain.shape[0]
    blocks = width // chans
    copies = lax.axis_size("z") // 2
    hid = w_out.shape[0] * lax.axis_size("y")
    swap = [(0, 1), (1, 0)]

    w_in = shifted(w_in)
    low, high = edges(floor_tokens[:3] + 1, floor_tokens[rows - 3 :] + 1)
    taps = depth_kernel.reshape(49, chans).T
    scale = lax.dynamic_slice_in_dim(layer_scale, lax.axis_index(CHAN) * chans, chans, 0)[:, None]
    gain = jnp.broadcast_to(norm_gain[:, None], (width, cols))
    grad_local = grad_out.transpose(0, 2, 1)

    tile = (rows, chans, cols)
    packed = (blocks, 2, chans, cols)
    x_local, send = call(
        functools.partial(first_kernel, copies),
        [(tile, BF16), (packed, BF16)],
        (floor_tokens, low, high, token_table.T, taps, scale, grad_local),
    )
    send, w_in = lax.optimization_barrier((send, w_in))
    w_out = shifted(w_out)
    weights = gathered(w_in)
    w_out, weights[1] = lax.optimization_barrier((w_out, weights[1]))
    weights = weights + gathered(w_out)
    own = lax.all_to_all(send, CHAN, 0, 0, tiled=True)
    own, *weights = lax.optimization_barrier((own, *weights))
    oth = lax.ppermute(own, "c", swap)
    keep, sib = call(
        middle_kernel,
        [(packed, F32), (packed, BF16)],
        (own, oth, gain, *weights),
        [VMEM] * 3 + [ANY] * 8,
        [
            pltpu.VMEM((width, hid), BF16),
            pltpu.VMEM((hid, width), BF16),
            pltpu.VMEM((width, 2 * cols), BF16),
            pltpu.VMEM((width, 2 * cols), BF16),
            pltpu.VMEM((width, 2 * cols), F32),
            pltpu.VMEM((width, 2 * cols), F32),
            pltpu.VMEM((hid, 2 * cols), BF16),
            pltpu.VMEM((hid, 2 * cols), BF16),
            pltpu.SemaphoreType.DMA((8,)),
        ],
        flops=8 * hid * width * 2 * cols,
        limit=40 << 20,
    )
    part = (keep + lax.ppermute(sib, "c", swap).astype(F32)).astype(BF16)
    got = lax.all_to_all(part, CHAN, 0, 0, tiled=True)
    edge = (3, chans, cols)
    block_out, gconv, low_side, high_side = call(
        functools.partial(sum_kernel, copies),
        [(tile, BF16), (tile, BF16), (edge, BF16), (edge, BF16)],
        (got, x_local, scale),
    )
    low, high = edges(low_side, high_side)
    (grad_embedded,) = call(last_kernel, [(tile, BF16)], (gconv, low, high, taps, grad_local))
    return block_out.transpose(0, 2, 1), grad_embedded.transpose(0, 2, 1)


def solution(mesh):
    chan, space = mesh.shape["chan"], mesh.shape["space"]
    grid = Mesh(mesh.devices.reshape(4, chan // 4, space // 4, 2, 2), AXES)
    placed = (
        P(SPACE, None),
        P(None, CHAN),
        P(None, None, CHAN),
        P(),
        P(),
        P(None, CHAN),
        P(CHAN, None),
        P(SPACE, None, CHAN),
    )
    return jax.shard_map(
        on_device,
        mesh=grid,
        in_specs=placed,
        out_specs=(P(SPACE, None, CHAN), P(SPACE, None, CHAN)),
        check_vma=False,
    )
```

```python
import functools
import itertools
import math

import jax
import jax.numpy as jnp
from jax import lax
from jax.experimental import pallas as pl
from jax.experimental.pallas import tpu as pltpu
from jax.sharding import Mesh, PartitionSpec as P

AXES = ("y", "z", "x", "h", "c")
CHAN = ("y", "z")
SPACE = ("x", "h", "c")
BF16, F32 = jnp.bfloat16, jnp.float32
VMEM = pl.BlockSpec(memory_space=pltpu.VMEM)
ANY = pl.BlockSpec(memory_space=pl.ANY)
ROOT = math.sqrt(2.0 / math.pi)


def edges(low_side, high_side):
    count = lax.axis_size(SPACE)
    forward = [(i, i + 1) for i in range(count - 1)]
    backward = [(j, i) for i, j in forward]
    return lax.ppermute(high_side, SPACE, forward), lax.ppermute(low_side, SPACE, backward)


def conv_rows(framed, taps_ref, flip, emit):
    rows = len(framed) - 6
    chans, cols = framed[0].shape
    lane = lax.broadcasted_iota(jnp.int32, (chans, cols), 1)
    totals = [jnp.zeros((chans, cols), F32) for _ in range(rows)]
    for b in range(7):
        step = (6 - b if flip else b) - 3
        taps = [
            jnp.broadcast_to(taps_ref[:, a * 7 + b : a * 7 + b + 1].astype(F32), (chans, cols))
            for a in range(7)
        ]
        inside = (lane + step >= 0) & (lane + step < cols)
        for i, tile in enumerate(framed):
            if step:
                tile = jnp.where(inside, pltpu.roll(tile, (-step) % cols, 1), 0.0)
            for a in range(7):
                r = i - (6 - a if flip else a)
                if 0 <= r < rows:
                    totals[r] = totals[r] + tile * taps[a]
    for r in range(rows):
        emit(r, totals[r])


def first_kernel(copies, tok_ref, low_ref, high_ref, table_ref, taps_ref, scale_ref, grad_ref, x_ref, send_ref):
    rows, cols = tok_ref.shape
    chans, vocab = table_ref.shape
    ident = lax.broadcasted_iota(jnp.int32, (vocab, cols), 0) + 1
    lines = [low_ref[i : i + 1] for i in range(3)]
    lines += [tok_ref[i : i + 1] + 1 for i in range(rows)]
    lines += [high_ref[i : i + 1] for i in range(3)]
    framed = []
    for line in lines:
        hot = (ident == line).astype(F32).astype(BF16)
        framed.append(jnp.dot(table_ref[...], hot, preferred_element_type=F32))
    for r in range(rows):
        x_ref[r] = framed[r + 3].astype(BF16)

    def targets(r):
        return [(r // 2) * 2 * copies + 2 * k + r % 2 for k in range(copies)]

    scale = jnp.broadcast_to(scale_ref[...], (chans, cols))
    for r in range(rows):
        mixed = (grad_ref[r].astype(F32) * scale).astype(BF16)
        for d in targets(r):
            send_ref[d, 1] = mixed

    def emit(r, total):
        total = total.astype(BF16)
        for d in targets(r):
            send_ref[d, 0] = total

    conv_rows(framed, taps_ref, False, emit)


def middle_kernel(
    own_ref, oth_ref, gain_ref, w0_ref, w1_ref, w2_ref, w3_ref,
    keep_ref, sib_ref,
    win, wout, scaled, gmix, normed, grads, act, gpre, sem,
):
    blocks, _, chans, cols = own_ref.shape
    width = blocks * chans
    hid = w0_ref.shape[1]
    pieces = [(ref.at[0], ref.at[1]) for ref in (w0_ref, w1_ref, w2_ref, w3_ref)]
    copies = []
    for i, (a, b) in enumerate(pieces):
        spot = pl.ds(i * hid, hid)
        copies.append(pltpu.make_async_copy(a, win.at[spot], sem.at[2 * i]))
        copies.append(pltpu.make_async_copy(b, wout.at[spot], sem.at[2 * i + 1]))
    for copy in copies:
        copy.start()

    def cell(s, t):
        return jnp.concatenate([own_ref[s, t], oth_ref[s, t]], axis=1)

    zero = jnp.zeros((chans, 2 * cols), F32)
    total = lax.fori_loop(0, blocks, lambda s, acc: acc + cell(s, 0).astype(F32), zero, unroll=8)
    mean = jnp.sum(total, axis=0, keepdims=True) * (1.0 / width)

    def square(s, acc):
        diff = cell(s, 0).astype(F32) - mean
        return acc + diff * diff

    total = lax.fori_loop(0, blocks, square, zero, unroll=8)
    inv_std = lax.rsqrt(jnp.sum(total, axis=0, keepdims=True) * (1.0 / width) + 1e-06)

    def norm(s, carry):
        spot = pl.ds(pl.multiple_of(s * chans, chans), chans)
        value = (cell(s, 0).astype(F32) - mean) * inv_std
        gain = gain_ref[spot, :]
        normed[spot, :] = value
        scaled[spot, :] = (value * jnp.concatenate([gain, gain], axis=1)).astype(BF16)
        gmix[spot, :] = cell(s, 1)
        return carry

    lax.fori_loop(0, blocks, norm, 0, unroll=4)
    for copy in copies:
        copy.wait()

    for i in range(len(pieces)):
        spot = pl.ds(i * hid, hid)
        pre = jnp.dot(win[spot, :], scaled[...], preferred_element_type=F32)
        gact = jnp.dot(wout[spot, :], gmix[...], preferred_element_type=F32)
        cube = pre * pre
        tanh = jnp.tanh(ROOT * (pre + 0.044715 * (cube * pre)))
        half = 0.5 * (1.0 + tanh)
        act[spot, :] = (pre * half).astype(BF16)
        slope = half + (0.5 * pre) * (1.0 - tanh * tanh) * (ROOT * (1.0 + 0.134145 * cube))
        gpre[spot, :] = (gact * slope).astype(BF16)

    group = 256
    per = group // chans
    sums = [jnp.zeros((1, 2 * cols), F32), jnp.zeros((1, 2 * cols), F32)]
    turned = (((0,), (0,)), ((), ()))
    for j in range(width // group):
        spot = pl.ds(j * group, group)
        gain = gain_ref[spot, :]
        part = lax.dot_general(win[:, spot], gpre[...], turned, preferred_element_type=F32)
        part = part * jnp.concatenate([gain, gain], axis=1)
        grads[spot, :] = part
        sums[0] = sums[0] + jnp.sum(part, axis=0, keepdims=True)
        sums[1] = sums[1] + jnp.sum(part * normed[spot, :], axis=0, keepdims=True)
        mix = lax.dot_general(wout[:, spot], act[...], turned, preferred_element_type=F32)
        for q in range(per):
            piece = mix[q * chans : (q + 1) * chans]
            keep_ref[j * per + q, 0] = piece[:, :cols]
            sib_ref[j * per + q, 0] = piece[:, cols:].astype(BF16)
    first, second = sums[0] * (1.0 / width), sums[1] * (1.0 / width)

    def finish(s, carry):
        spot = pl.ds(pl.multiple_of(s * chans, chans), chans)
        piece = inv_std * (grads[spot, :] - first - normed[spot, :] * second)
        keep_ref[s, 1] = piece[:, :cols]
        sib_ref[s, 1] = piece[:, cols:].astype(BF16)
        return carry

    lax.fori_loop(0, blocks, finish, 0, unroll=4)


def sum_kernel(copies, got_ref, x_ref, scale_ref, out_ref, gconv_ref, low_ref, high_ref):
    rows, chans, cols = x_ref.shape
    scale = jnp.broadcast_to(scale_ref[...], (chans, cols))
    for r in range(rows):
        base = (r // 2) * 2 * copies + r % 2
        mix = got_ref[base, 0].astype(F32)
        conv = got_ref[base, 1].astype(F32)
        for k in range(1, copies):
            mix = mix + got_ref[base + 2 * k, 0].astype(F32)
            conv = conv + got_ref[base + 2 * k, 1].astype(F32)
        out_ref[r] = (x_ref[r].astype(F32) + scale * mix).astype(BF16)
        conv = conv.astype(BF16)
        gconv_ref[r] = conv
        if r < 3:
            low_ref[r] = conv
        if r >= rows - 3:
            high_ref[r - rows + 3] = conv


def last_kernel(gconv_ref, low_ref, high_ref, taps_ref, grad_ref, out_ref):
    rows = gconv_ref.shape[0]
    framed = [low_ref[i].astype(F32) for i in range(3)]
    framed += [gconv_ref[i].astype(F32) for i in range(rows)]
    framed += [high_ref[i].astype(F32) for i in range(3)]

    def emit(r, total):
        out_ref[r] = (grad_ref[r].astype(F32) + total).astype(BF16)

    conv_rows(framed, taps_ref, True, emit)


def call(body, outs, args, specs=None, scratch=(), flops=1 << 20, limit=32 << 20):
    outs = [jax.ShapeDtypeStruct(s, d) for s, d in outs]
    return pl.pallas_call(
        body,
        out_shape=outs,
        in_specs=specs or [VMEM] * len(args),
        out_specs=[VMEM] * len(outs),
        scratch_shapes=list(scratch),
        compiler_params=pltpu.CompilerParams(vmem_limit_bytes=limit),
        cost_estimate=pl.CostEstimate(flops=flops, bytes_accessed=4 << 20, transcendentals=0),
    )(*args)


def shifted(shard):
    ny, nz, nx, nh, nc = (lax.axis_size(a) for a in AXES)
    count = ny * nh

    def place(y, z, x, h, c):
        return (((y * nz + z) * nx + x) * nh + h) * nc + c

    pairs = []
    for y, z, x, h, c in itertools.product(*[range(n) for n in (ny, nz, nx, nh, nc)]):
        turn = x % ny
        if 2 * turn > ny or (2 * turn == ny and c):
            turn -= ny
        spot = (h * ny + y + turn) % count
        other = (z, c) if z % 2 == c else (z ^ 1, 1 - c)
        pairs.append((place(spot % ny, other[0], x, spot // ny, other[1]), place(y, z, x, h, c)))
    return lax.ppermute(shard, AXES, pairs)


def gathered(shard):
    nx = lax.axis_size("x")
    others = [lax.ppermute(shard, "x", [((i + k) % nx, i) for i in range(nx)]) for k in (2, 1, 3)]
    return [shard, *others]


def on_device(
    floor_tokens, token_table, depth_kernel, norm_gain, layer_scale, w_in, w_out, grad_out
):
    rows, cols = floor_tokens.shape
    chans = depth_kernel.shape[2]
    width = norm_gain.shape[0]
    blocks = width // chans
    copies = lax.axis_size("z") // 2
    hid = w_out.shape[0] * lax.axis_size("y")
    swap = [(0, 1), (1, 0)]

    both = shifted(jnp.stack([w_in.T, w_out]))
    low, high = edges(floor_tokens[:3] + 1, floor_tokens[rows - 3 :] + 1)
    taps = depth_kernel.reshape(49, chans).T
    scale = lax.dynamic_slice_in_dim(layer_scale, lax.axis_index(CHAN) * chans, chans, 0)[:, None]
    gain = jnp.broadcast_to(norm_gain[:, None], (width, cols))
    grad_local = grad_out.transpose(0, 2, 1)

    tile = (rows, chans, cols)
    packed = (blocks, 2, chans, cols)
    x_local, send = call(
        functools.partial(first_kernel, copies),
        [(tile, BF16), (packed, BF16)],
        (floor_tokens, low, high, token_table.T, taps, scale, grad_local),
    )
    send, both = lax.optimization_barrier((send, both))
    weights = gathered(both)
    own = lax.all_to_all(send, CHAN, 0, 0, tiled=True)
    oth = lax.ppermute(own, "c", swap)
    keep, sib = call(
        middle_kernel,
        [(packed, F32), (packed, BF16)],
        (own, oth, gain, *weights),
        [VMEM] * 3 + [ANY] * 4,
        [
            pltpu.VMEM((hid, width), BF16),
            pltpu.VMEM((hid, width), BF16),
            pltpu.VMEM((width, 2 * cols), BF16),
            pltpu.VMEM((width, 2 * cols), BF16),
            pltpu.VMEM((width, 2 * cols), F32),
            pltpu.VMEM((width, 2 * cols), F32),
            pltpu.VMEM((hid, 2 * cols), BF16),
            pltpu.VMEM((hid, 2 * cols), BF16),
            pltpu.SemaphoreType.DMA((8,)),
        ],
        flops=8 * hid * width * 2 * cols,
        limit=40 << 20,
    )
    part = (keep + lax.ppermute(sib, "c", swap).astype(F32)).astype(BF16)
    got = lax.all_to_all(part, CHAN, 0, 0, tiled=True)
    edge = (3, chans, cols)
    block_out, gconv, low_side, high_side = call(
        functools.partial(sum_kernel, copies),
        [(tile, BF16), (tile, BF16), (edge, BF16), (edge, BF16)],
        (got, x_local, scale),
    )
    low, high = edges(low_side, high_side)
    (grad_embedded,) = call(last_kernel, [(tile, BF16)], (gconv, low, high, taps, grad_local))
    return block_out.transpose(0, 2, 1), grad_embedded.transpose(0, 2, 1)


def solution(mesh):
    chan, space = mesh.shape["chan"], mesh.shape["space"]
    grid = Mesh(mesh.devices.reshape(4, chan // 4, space // 4, 2, 2), AXES)
    placed = (
        P(SPACE, None),
        P(None, CHAN),
        P(None, None, CHAN),
        P(),
        P(),
        P(None, CHAN),
        P(CHAN, None),
        P(SPACE, None, CHAN),
    )
    return jax.shard_map(
        on_device,
        mesh=grid,
        in_specs=placed,
        out_specs=(P(SPACE, None, CHAN), P(SPACE, None, CHAN)),
        check_vma=False,
    )
```

```python
import functools
import itertools
import math

import jax
import jax.numpy as jnp
from jax import lax
from jax.experimental import pallas as pl
from jax.experimental.pallas import tpu as pltpu
from jax.sharding import Mesh, PartitionSpec as P

AXES = ("y", "z", "x", "h", "c")
CHAN = ("y", "z")
SPACE = ("x", "h", "c")
BF16, F32 = jnp.bfloat16, jnp.float32
VMEM = pl.BlockSpec(memory_space=pltpu.VMEM)
ANY = pl.BlockSpec(memory_space=pl.ANY)
ROOT = math.sqrt(2.0 / math.pi)


def edges(low_side, high_side):
    count = lax.axis_size(SPACE)
    forward = [(i, i + 1) for i in range(count - 1)]
    backward = [(j, i) for i, j in forward]
    return lax.ppermute(high_side, SPACE, forward), lax.ppermute(low_side, SPACE, backward)


def conv_rows(framed, taps_ref, flip, emit):
    rows = len(framed) - 6
    chans, cols = framed[0].shape
    lane = lax.broadcasted_iota(jnp.int32, (chans, cols), 1)
    totals = [jnp.zeros((chans, cols), F32) for _ in range(rows)]
    for b in range(7):
        step = (6 - b if flip else b) - 3
        taps = [
            jnp.broadcast_to(taps_ref[:, a * 7 + b : a * 7 + b + 1].astype(F32), (chans, cols))
            for a in range(7)
        ]
        inside = (lane + step >= 0) & (lane + step < cols)
        for i, tile in enumerate(framed):
            if step:
                tile = jnp.where(inside, pltpu.roll(tile, (-step) % cols, 1), 0.0)
            for a in range(7):
                r = i - (6 - a if flip else a)
                if 0 <= r < rows:
                    totals[r] = totals[r] + tile * taps[a]
    for r in range(rows):
        emit(r, totals[r])


def first_kernel(copies, tok_ref, low_ref, high_ref, table_ref, taps_ref, scale_ref, grad_ref, x_ref, send_ref):
    rows, cols = tok_ref.shape
    chans, vocab = table_ref.shape
    ident = lax.broadcasted_iota(jnp.int32, (vocab, cols), 0) + 1
    lines = [low_ref[i : i + 1] for i in range(3)]
    lines += [tok_ref[i : i + 1] + 1 for i in range(rows)]
    lines += [high_ref[i : i + 1] for i in range(3)]
    framed = []
    for line in lines:
        hot = (ident == line).astype(F32).astype(BF16)
        framed.append(jnp.dot(table_ref[...], hot, preferred_element_type=F32))
    for r in range(rows):
        x_ref[r] = framed[r + 3].astype(BF16)

    def targets(r):
        return [(r // 2) * 2 * copies + 2 * k + r % 2 for k in range(copies)]

    scale = jnp.broadcast_to(scale_ref[...], (chans, cols))
    for r in range(rows):
        mixed = (grad_ref[r].astype(F32) * scale).astype(BF16)
        for d in targets(r):
            send_ref[d, 1] = mixed

    def emit(r, total):
        total = total.astype(BF16)
        for d in targets(r):
            send_ref[d, 0] = total

    conv_rows(framed, taps_ref, False, emit)


def middle_kernel(
    own_ref, oth_ref, gain_ref, in_ref, o0_ref, o1_ref, o2_ref, o3_ref,
    keep_ref, sib_ref,
    win, wout, scaled, gmix, normed, grads, act, gpre, sem,
):
    blocks, _, chans, cols = own_ref.shape
    width = blocks * chans
    hid = o0_ref.shape[0]
    pieces = (o0_ref, o1_ref, o2_ref, o3_ref)
    copies = [pltpu.make_async_copy(in_ref, win, sem.at[0])]
    for i, piece in enumerate(pieces):
        copies.append(pltpu.make_async_copy(piece, wout.at[pl.ds(i * hid, hid)], sem.at[i + 1]))
    for copy in copies:
        copy.start()

    def cell(s, t):
        return jnp.concatenate([own_ref[s, t], oth_ref[s, t]], axis=1)

    zero = jnp.zeros((chans, 2 * cols), F32)
    total = lax.fori_loop(0, blocks, lambda s, acc: acc + cell(s, 0).astype(F32), zero, unroll=8)
    mean = jnp.sum(total, axis=0, keepdims=True) * (1.0 / width)

    def square(s, acc):
        diff = cell(s, 0).astype(F32) - mean
        return acc + diff * diff

    total = lax.fori_loop(0, blocks, square, zero, unroll=8)
    inv_std = lax.rsqrt(jnp.sum(total, axis=0, keepdims=True) * (1.0 / width) + 1e-06)

    def norm(s, carry):
        spot = pl.ds(pl.multiple_of(s * chans, chans), chans)
        value = (cell(s, 0).astype(F32) - mean) * inv_std
        gain = gain_ref[spot, :]
        normed[spot, :] = value
        scaled[spot, :] = (value * jnp.concatenate([gain, gain], axis=1)).astype(BF16)
        gmix[spot, :] = cell(s, 1)
        return carry

    lax.fori_loop(0, blocks, norm, 0, unroll=4)
    for copy in copies:
        copy.wait()

    turned = (((0,), (0,)), ((), ()))
    for i in range(len(pieces)):
        spot = pl.ds(i * hid, hid)
        pre = lax.dot_general(win[:, spot], scaled[...], turned, preferred_element_type=F32)
        gact = jnp.dot(wout[spot, :], gmix[...], preferred_element_type=F32)
        cube = pre * pre
        tanh = jnp.tanh(ROOT * (pre + 0.044715 * (cube * pre)))
        half = 0.5 * (1.0 + tanh)
        act[spot, :] = (pre * half).astype(BF16)
        slope = half + (0.5 * pre) * (1.0 - tanh * tanh) * (ROOT * (1.0 + 0.134145 * cube))
        gpre[spot, :] = (gact * slope).astype(BF16)

    group = 256
    per = group // chans
    sums = [jnp.zeros((1, 2 * cols), F32), jnp.zeros((1, 2 * cols), F32)]
    for j in range(width // group):
        spot = pl.ds(j * group, group)
        gain = gain_ref[spot, :]
        part = jnp.dot(win[spot, :], gpre[...], preferred_element_type=F32)
        part = part * jnp.concatenate([gain, gain], axis=1)
        grads[spot, :] = part
        sums[0] = sums[0] + jnp.sum(part, axis=0, keepdims=True)
        sums[1] = sums[1] + jnp.sum(part * normed[spot, :], axis=0, keepdims=True)
        mix = lax.dot_general(wout[:, spot], act[...], turned, preferred_element_type=F32)
        for q in range(per):
            piece = mix[q * chans : (q + 1) * chans]
            keep_ref[j * per + q, 0] = piece[:, :cols]
            sib_ref[j * per + q, 0] = piece[:, cols:].astype(BF16)
    first, second = sums[0] * (1.0 / width), sums[1] * (1.0 / width)

    def finish(s, carry):
        spot = pl.ds(pl.multiple_of(s * chans, chans), chans)
        piece = inv_std * (grads[spot, :] - first - normed[spot, :] * second)
        keep_ref[s, 1] = piece[:, :cols]
        sib_ref[s, 1] = piece[:, cols:].astype(BF16)
        return carry

    lax.fori_loop(0, blocks, finish, 0, unroll=4)


def sum_kernel(copies, got_ref, x_ref, scale_ref, out_ref, gconv_ref, low_ref, high_ref):
    rows, chans, cols = x_ref.shape
    scale = jnp.broadcast_to(scale_ref[...], (chans, cols))
    for r in range(rows):
        base = (r // 2) * 2 * copies + r % 2
        mix = got_ref[base, 0].astype(F32)
        conv = got_ref[base, 1].astype(F32)
        for k in range(1, copies):
            mix = mix + got_ref[base + 2 * k, 0].astype(F32)
            conv = conv + got_ref[base + 2 * k, 1].astype(F32)
        out_ref[r] = (x_ref[r].astype(F32) + scale * mix).astype(BF16)
        conv = conv.astype(BF16)
        gconv_ref[r] = conv
        if r < 3:
            low_ref[r] = conv
        if r >= rows - 3:
            high_ref[r - rows + 3] = conv


def last_kernel(gconv_ref, low_ref, high_ref, taps_ref, grad_ref, out_ref):
    rows = gconv_ref.shape[0]
    framed = [low_ref[i].astype(F32) for i in range(3)]
    framed += [gconv_ref[i].astype(F32) for i in range(rows)]
    framed += [high_ref[i].astype(F32) for i in range(3)]

    def emit(r, total):
        out_ref[r] = (grad_ref[r].astype(F32) + total).astype(BF16)

    conv_rows(framed, taps_ref, True, emit)


def call(body, outs, args, specs=None, scratch=(), flops=1 << 20, limit=32 << 20):
    outs = [jax.ShapeDtypeStruct(s, d) for s, d in outs]
    return pl.pallas_call(
        body,
        out_shape=outs,
        in_specs=specs or [VMEM] * len(args),
        out_specs=[VMEM] * len(outs),
        scratch_shapes=list(scratch),
        compiler_params=pltpu.CompilerParams(vmem_limit_bytes=limit),
        cost_estimate=pl.CostEstimate(flops=flops, bytes_accessed=4 << 20, transcendentals=0),
    )(*args)


def moved(shard, turn_of):
    ny, nz, nx, nh, nc = (lax.axis_size(a) for a in AXES)

    def place(y, z, x, h, c):
        return (((y * nz + z) * nx + x) * nh + h) * nc + c

    pairs = []
    for y, z, x, h, c in itertools.product(*[range(n) for n in (ny, nz, nx, nh, nc)]):
        spot = (h * ny + y + turn_of(x, c)) % (ny * nh)
        other = (z, c) if z % 2 == c else (z ^ 1, 1 - c)
        pairs.append((place(spot % ny, other[0], x, spot // ny, other[1]), place(y, z, x, h, c)))
    return lax.ppermute(shard, AXES, pairs)


def turns(k, c):
    return (0, 1, -2 if c else 2, -1)[k]


def from_ring(shard, k):
    nh, ny = lax.axis_size("h"), lax.axis_size("y")
    ring = [y * nh + h for h in range(nh) for y in range(ny)]
    count = len(ring)
    pairs = [
        (ring[(i + turns(k, c)) % count] * 2 + c, ring[i] * 2 + c) for i in range(count) for c in range(2)
    ]
    return lax.ppermute(shard, ("y", "h", "c"), pairs)


def on_device(
    floor_tokens, token_table, depth_kernel, norm_gain, layer_scale, w_in, w_out, grad_out
):
    rows, cols = floor_tokens.shape
    chans = depth_kernel.shape[2]
    width = norm_gain.shape[0]
    blocks = width // chans
    copies = lax.axis_size("z") // 2
    hid = w_out.shape[0] * lax.axis_size("y")
    swap = [(0, 1), (1, 0)]

    w_in = moved(w_in, lambda x, c: turns(x, c))
    w_out = moved(w_out, lambda x, c: 0)
    low, high = edges(floor_tokens[:3] + 1, floor_tokens[rows - 3 :] + 1)
    taps = depth_kernel.reshape(49, chans).T
    scale = lax.dynamic_slice_in_dim(layer_scale, lax.axis_index(CHAN) * chans, chans, 0)[:, None]
    gain = jnp.broadcast_to(norm_gain[:, None], (width, cols))
    grad_local = grad_out.transpose(0, 2, 1)

    tile = (rows, chans, cols)
    packed = (blocks, 2, chans, cols)
    x_local, send = call(
        functools.partial(first_kernel, copies),
        [(tile, BF16), (packed, BF16)],
        (floor_tokens, low, high, token_table.T, taps, scale, grad_local),
    )
    send, w_in, w_out = lax.optimization_barrier((send, w_in, w_out))
    w_in = lax.all_gather(w_in, "x", axis=1, tiled=True)
    weights = [w_in, w_out, *[from_ring(w_out, k) for k in (1, 2, 3)]]
    own = lax.all_to_all(send, CHAN, 0, 0, tiled=True)
    own, *weights = lax.optimization_barrier((own, *weights))
    oth = lax.ppermute(own, "c", swap)
    keep, sib = call(
        middle_kernel,
        [(packed, F32), (packed, BF16)],
        (own, oth, gain, *weights),
        [VMEM] * 3 + [ANY] * 5,
        [
            pltpu.VMEM((width, hid), BF16),
            pltpu.VMEM((hid, width), BF16),
            pltpu.VMEM((width, 2 * cols), BF16),
            pltpu.VMEM((width, 2 * cols), BF16),
            pltpu.VMEM((width, 2 * cols), F32),
            pltpu.VMEM((width, 2 * cols), F32),
            pltpu.VMEM((hid, 2 * cols), BF16),
            pltpu.VMEM((hid, 2 * cols), BF16),
            pltpu.SemaphoreType.DMA((5,)),
        ],
        flops=8 * hid * width * 2 * cols,
        limit=40 << 20,
    )
    part = (keep + lax.ppermute(sib, "c", swap).astype(F32)).astype(BF16)
    got = lax.all_to_all(part, CHAN, 0, 0, tiled=True)
    edge = (3, chans, cols)
    block_out, gconv, low_side, high_side = call(
        functools.partial(sum_kernel, copies),
        [(tile, BF16), (tile, BF16), (edge, BF16), (edge, BF16)],
        (got, x_local, scale),
    )
    low, high = edges(low_side, high_side)
    (grad_embedded,) = call(last_kernel, [(tile, BF16)], (gconv, low, high, taps, grad_local))
    return block_out.transpose(0, 2, 1), grad_embedded.transpose(0, 2, 1)


def solution(mesh):
    chan, space = mesh.shape["chan"], mesh.shape["space"]
    grid = Mesh(mesh.devices.reshape(4, chan // 4, space // 4, 2, 2), AXES)
    placed = (
        P(SPACE, None),
        P(None, CHAN),
        P(None, None, CHAN),
        P(),
        P(),
        P(None, CHAN),
        P(CHAN, None),
        P(SPACE, None, CHAN),
    )
    return jax.shard_map(
        on_device,
        mesh=grid,
        in_specs=placed,
        out_specs=(P(SPACE, None, CHAN), P(SPACE, None, CHAN)),
        check_vma=False,
    )
```

```python
import functools
import itertools
import math

import jax
import jax.numpy as jnp
from jax import lax
from jax.experimental import pallas as pl
from jax.experimental.pallas import tpu as pltpu
from jax.sharding import Mesh, PartitionSpec as P

AXES = ("y", "z", "x", "h", "c")
CHAN = ("y", "z")
SPACE = ("x", "h", "c")
BF16, F32 = jnp.bfloat16, jnp.float32
VMEM = pl.BlockSpec(memory_space=pltpu.VMEM)
ANY = pl.BlockSpec(memory_space=pl.ANY)
ROOT = math.sqrt(2.0 / math.pi)


def edges(low_side, high_side):
    count = lax.axis_size(SPACE)
    forward = [(i, i + 1) for i in range(count - 1)]
    backward = [(j, i) for i, j in forward]
    return lax.ppermute(high_side, SPACE, forward), lax.ppermute(low_side, SPACE, backward)


def conv_rows(framed, taps_ref, flip, emit):
    rows = len(framed) - 6
    chans, cols = framed[0].shape
    lane = lax.broadcasted_iota(jnp.int32, (chans, cols), 1)
    totals = [jnp.zeros((chans, cols), F32) for _ in range(rows)]
    for b in range(7):
        step = (6 - b if flip else b) - 3
        taps = [
            jnp.broadcast_to(taps_ref[:, a * 7 + b : a * 7 + b + 1].astype(F32), (chans, cols))
            for a in range(7)
        ]
        inside = (lane + step >= 0) & (lane + step < cols)
        for i, tile in enumerate(framed):
            if step:
                tile = jnp.where(inside, pltpu.roll(tile, (-step) % cols, 1), 0.0)
            for a in range(7):
                r = i - (6 - a if flip else a)
                if 0 <= r < rows:
                    totals[r] = totals[r] + tile * taps[a]
    for r in range(rows):
        emit(r, totals[r])


def first_kernel(copies, tok_ref, low_ref, high_ref, table_ref, taps_ref, scale_ref, grad_ref, x_ref, send_ref):
    rows, cols = tok_ref.shape
    chans, vocab = table_ref.shape
    ident = lax.broadcasted_iota(jnp.int32, (vocab, cols), 0) + 1
    lines = [low_ref[i : i + 1] for i in range(3)]
    lines += [tok_ref[i : i + 1] + 1 for i in range(rows)]
    lines += [high_ref[i : i + 1] for i in range(3)]
    framed = []
    for line in lines:
        hot = (ident == line).astype(F32).astype(BF16)
        framed.append(jnp.dot(table_ref[...], hot, preferred_element_type=F32))
    for r in range(rows):
        x_ref[r] = framed[r + 3].astype(BF16)

    def targets(r):
        return [(r // 2) * 2 * copies + 2 * k + r % 2 for k in range(copies)]

    scale = jnp.broadcast_to(scale_ref[...], (chans, cols))
    for r in range(rows):
        mixed = (grad_ref[r].astype(F32) * scale).astype(BF16)
        for d in targets(r):
            send_ref[d, 1] = mixed

    def emit(r, total):
        total = total.astype(BF16)
        for d in targets(r):
            send_ref[d, 0] = total

    conv_rows(framed, taps_ref, False, emit)


def middle_kernel(
    own_ref, oth_ref, gain_ref, w0_ref, w1_ref, w2_ref, w3_ref,
    keep_ref, sib_ref,
    win, wout, scaled, gmix, normed, grads, act, gpre, sem,
):
    blocks, _, chans, cols = own_ref.shape
    width = blocks * chans
    hid = w0_ref.shape[1]
    pieces = [(ref.at[0], ref.at[1]) for ref in (w0_ref, w1_ref, w2_ref, w3_ref)]
    copies = []
    for i, (a, b) in enumerate(pieces):
        spot = pl.ds(i * hid, hid)
        copies.append(pltpu.make_async_copy(a, win.at[spot], sem.at[2 * i]))
        copies.append(pltpu.make_async_copy(b, wout.at[spot], sem.at[2 * i + 1]))
    for copy in copies:
        copy.start()

    def cell(s, t):
        return jnp.concatenate([own_ref[s, t], oth_ref[s, t]], axis=1)

    zero = jnp.zeros((chans, 2 * cols), F32)
    total = lax.fori_loop(0, blocks, lambda s, acc: acc + cell(s, 0).astype(F32), zero, unroll=8)
    mean = jnp.sum(total, axis=0, keepdims=True) * (1.0 / width)

    def square(s, acc):
        diff = cell(s, 0).astype(F32) - mean
        return acc + diff * diff

    total = lax.fori_loop(0, blocks, square, zero, unroll=8)
    inv_std = lax.rsqrt(jnp.sum(total, axis=0, keepdims=True) * (1.0 / width) + 1e-06)

    def norm(s, carry):
        spot = pl.ds(pl.multiple_of(s * chans, chans), chans)
        value = (cell(s, 0).astype(F32) - mean) * inv_std
        gain = gain_ref[spot, :]
        normed[spot, :] = value
        scaled[spot, :] = (value * jnp.concatenate([gain, gain], axis=1)).astype(BF16)
        gmix[spot, :] = cell(s, 1)
        return carry

    lax.fori_loop(0, blocks, norm, 0, unroll=4)
    for copy in copies:
        copy.wait()

    for i in range(len(pieces)):
        spot = pl.ds(i * hid, hid)
        pre = jnp.dot(win[spot, :], scaled[...], preferred_element_type=F32)
        gact = jnp.dot(wout[spot, :], gmix[...], preferred_element_type=F32)
        cube = pre * pre
        tanh = jnp.tanh(ROOT * (pre + 0.044715 * (cube * pre)))
        half = 0.5 * (1.0 + tanh)
        act[spot, :] = (pre * half).astype(BF16)
        slope = half + (0.5 * pre) * (1.0 - tanh * tanh) * (ROOT * (1.0 + 0.134145 * cube))
        gpre[spot, :] = (gact * slope).astype(BF16)

    group = 256
    per = group // chans
    sums = [jnp.zeros((1, 2 * cols), F32), jnp.zeros((1, 2 * cols), F32)]
    turned = (((0,), (0,)), ((), ()))
    for j in range(width // group):
        spot = pl.ds(j * group, group)
        gain = gain_ref[spot, :]
        part = lax.dot_general(win[:, spot], gpre[...], turned, preferred_element_type=F32)
        part = part * jnp.concatenate([gain, gain], axis=1)
        grads[spot, :] = part
        sums[0] = sums[0] + jnp.sum(part, axis=0, keepdims=True)
        sums[1] = sums[1] + jnp.sum(part * normed[spot, :], axis=0, keepdims=True)
        mix = lax.dot_general(wout[:, spot], act[...], turned, preferred_element_type=F32)
        for q in range(per):
            piece = mix[q * chans : (q + 1) * chans]
            keep_ref[j * per + q, 0] = piece[:, :cols]
            sib_ref[j * per + q, 0] = piece[:, cols:].astype(BF16)
    first, second = sums[0] * (1.0 / width), sums[1] * (1.0 / width)

    def finish(s, carry):
        spot = pl.ds(pl.multiple_of(s * chans, chans), chans)
        piece = inv_std * (grads[spot, :] - first - normed[spot, :] * second)
        keep_ref[s, 1] = piece[:, :cols]
        sib_ref[s, 1] = piece[:, cols:].astype(BF16)
        return carry

    lax.fori_loop(0, blocks, finish, 0, unroll=4)


def sum_kernel(copies, got_ref, x_ref, scale_ref, out_ref, gconv_ref, low_ref, high_ref):
    rows, chans, cols = x_ref.shape
    scale = jnp.broadcast_to(scale_ref[...], (chans, cols))
    for r in range(rows):
        base = (r // 2) * 2 * copies + r % 2
        mix = got_ref[base, 0].astype(F32)
        conv = got_ref[base, 1].astype(F32)
        for k in range(1, copies):
            mix = mix + got_ref[base + 2 * k, 0].astype(F32)
            conv = conv + got_ref[base + 2 * k, 1].astype(F32)
        out_ref[r] = (x_ref[r].astype(F32) + scale * mix).astype(BF16)
        conv = conv.astype(BF16)
        gconv_ref[r] = conv
        if r < 3:
            low_ref[r] = conv
        if r >= rows - 3:
            high_ref[r - rows + 3] = conv


def last_kernel(gconv_ref, low_ref, high_ref, taps_ref, grad_ref, out_ref):
    rows = gconv_ref.shape[0]
    framed = [low_ref[i].astype(F32) for i in range(3)]
    framed += [gconv_ref[i].astype(F32) for i in range(rows)]
    framed += [high_ref[i].astype(F32) for i in range(3)]

    def emit(r, total):
        out_ref[r] = (grad_ref[r].astype(F32) + total).astype(BF16)

    conv_rows(framed, taps_ref, True, emit)


def call(body, outs, args, specs=None, scratch=(), flops=1 << 20, limit=32 << 20):
    outs = [jax.ShapeDtypeStruct(s, d) for s, d in outs]
    return pl.pallas_call(
        body,
        out_shape=outs,
        in_specs=specs or [VMEM] * len(args),
        out_specs=[VMEM] * len(outs),
        scratch_shapes=list(scratch),
        compiler_params=pltpu.CompilerParams(vmem_limit_bytes=limit),
        cost_estimate=pl.CostEstimate(flops=flops, bytes_accessed=4 << 20, transcendentals=0),
    )(*args)


def moved(shard, k):
    ny, nz, nx, nh, nc = (lax.axis_size(a) for a in AXES)

    def place(y, z, x, h, c):
        return (((y * nz + z) * nx + x) * nh + h) * nc + c

    pairs = []
    for y, z, x, h, c in itertools.product(*[range(n) for n in (ny, nz, nx, nh, nc)]):
        spot = (h * ny + y + turns(k, c)) % (ny * nh)
        other = (z, c) if z % 2 == c else (z ^ 1, 1 - c)
        pairs.append((place(spot % ny, other[0], x, spot // ny, other[1]), place(y, z, x, h, c)))
    return lax.ppermute(shard, AXES, pairs)


def turns(k, c):
    return (0, 1, -2 if c else 2, -1)[k]


def from_ring(shard, k):
    nh, ny = lax.axis_size("h"), lax.axis_size("y")
    ring = [y * nh + h for h in range(nh) for y in range(ny)]
    count = len(ring)
    pairs = [
        (ring[(i + turns(k, c)) % count] * 2 + c, ring[i] * 2 + c) for i in range(count) for c in range(2)
    ]
    return lax.ppermute(shard, ("y", "h", "c"), pairs)


def on_device(
    floor_tokens, token_table, depth_kernel, norm_gain, layer_scale, w_in, w_out, grad_out
):
    rows, cols = floor_tokens.shape
    chans = depth_kernel.shape[2]
    width = norm_gain.shape[0]
    blocks = width // chans
    copies = lax.axis_size("z") // 2
    hid = w_out.shape[0] * lax.axis_size("y")
    swap = [(0, 1), (1, 0)]

    both = jnp.stack([w_in.T, w_out])
    near, far = moved(both, 0), moved(both, 2)
    low, high = edges(floor_tokens[:3] + 1, floor_tokens[rows - 3 :] + 1)
    taps = depth_kernel.reshape(49, chans).T
    scale = lax.dynamic_slice_in_dim(layer_scale, lax.axis_index(CHAN) * chans, chans, 0)[:, None]
    gain = jnp.broadcast_to(norm_gain[:, None], (width, cols))
    grad_local = grad_out.transpose(0, 2, 1)

    tile = (rows, chans, cols)
    packed = (blocks, 2, chans, cols)
    x_local, send = call(
        functools.partial(first_kernel, copies),
        [(tile, BF16), (packed, BF16)],
        (floor_tokens, low, high, token_table.T, taps, scale, grad_local),
    )
    send, near, far = lax.optimization_barrier((send, near, far))
    weights = [near, far, from_ring(near, 1), from_ring(near, 3)]
    own = lax.all_to_all(send, CHAN, 0, 0, tiled=True)
    oth = lax.ppermute(own, "c", swap)
    keep, sib = call(
        middle_kernel,
        [(packed, F32), (packed, BF16)],
        (own, oth, gain, *weights),
        [VMEM] * 3 + [ANY] * 4,
        [
            pltpu.VMEM((hid, width), BF16),
            pltpu.VMEM((hid, width), BF16),
            pltpu.VMEM((width, 2 * cols), BF16),
            pltpu.VMEM((width, 2 * cols), BF16),
            pltpu.VMEM((width, 2 * cols), F32),
            pltpu.VMEM((width, 2 * cols), F32),
            pltpu.VMEM((hid, 2 * cols), BF16),
            pltpu.VMEM((hid, 2 * cols), BF16),
            pltpu.SemaphoreType.DMA((8,)),
        ],
        flops=8 * hid * width * 2 * cols,
        limit=40 << 20,
    )
    part = (keep + lax.ppermute(sib, "c", swap).astype(F32)).astype(BF16)
    got = lax.all_to_all(part, CHAN, 0, 0, tiled=True)
    edge = (3, chans, cols)
    block_out, gconv, low_side, high_side = call(
        functools.partial(sum_kernel, copies),
        [(tile, BF16), (tile, BF16), (edge, BF16), (edge, BF16)],
        (got, x_local, scale),
    )
    low, high = edges(low_side, high_side)
    (grad_embedded,) = call(last_kernel, [(tile, BF16)], (gconv, low, high, taps, grad_local))
    return block_out.transpose(0, 2, 1), grad_embedded.transpose(0, 2, 1)


def solution(mesh):
    chan, space = mesh.shape["chan"], mesh.shape["space"]
    grid = Mesh(mesh.devices.reshape(4, chan // 4, space // 4, 2, 2), AXES)
    placed = (
        P(SPACE, None),
        P(None, CHAN),
        P(None, None, CHAN),
        P(),
        P(),
        P(None, CHAN),
        P(CHAN, None),
        P(SPACE, None, CHAN),
    )
    return jax.shard_map(
        on_device,
        mesh=grid,
        in_specs=placed,
        out_specs=(P(SPACE, None, CHAN), P(SPACE, None, CHAN)),
        check_vma=False,
    )
```

```python
import functools
import itertools
import math

import jax
import jax.numpy as jnp
from jax import lax
from jax.experimental import pallas as pl
from jax.experimental.pallas import tpu as pltpu
from jax.sharding import Mesh, PartitionSpec as P

AXES = ("y", "z", "x", "h", "c")
CHAN = ("y", "z")
SPACE = ("x", "h", "c")
BF16, F32 = jnp.bfloat16, jnp.float32
VMEM = pl.BlockSpec(memory_space=pltpu.VMEM)
ANY = pl.BlockSpec(memory_space=pl.ANY)
ROOT = math.sqrt(2.0 / math.pi)


def edges(low_side, high_side):
    count = lax.axis_size(SPACE)
    forward = [(i, i + 1) for i in range(count - 1)]
    backward = [(j, i) for i, j in forward]
    return lax.ppermute(high_side, SPACE, forward), lax.ppermute(low_side, SPACE, backward)


def conv_rows(framed, taps_ref, flip, emit):
    rows = len(framed) - 6
    chans, cols = framed[0].shape
    lane = lax.broadcasted_iota(jnp.int32, (chans, cols), 1)
    totals = [jnp.zeros((chans, cols), F32) for _ in range(rows)]
    for b in range(7):
        step = (6 - b if flip else b) - 3
        taps = [
            jnp.broadcast_to(taps_ref[:, a * 7 + b : a * 7 + b + 1].astype(F32), (chans, cols))
            for a in range(7)
        ]
        inside = (lane + step >= 0) & (lane + step < cols)
        for i, tile in enumerate(framed):
            if step:
                tile = jnp.where(inside, pltpu.roll(tile, (-step) % cols, 1), 0.0)
            for a in range(7):
                r = i - (6 - a if flip else a)
                if 0 <= r < rows:
                    totals[r] = totals[r] + tile * taps[a]
    for r in range(rows):
        emit(r, totals[r])


def first_kernel(copies, tok_ref, low_ref, high_ref, table_ref, taps_ref, scale_ref, grad_ref, x_ref, send_ref):
    rows, cols = tok_ref.shape
    chans, vocab = table_ref.shape
    ident = lax.broadcasted_iota(jnp.int32, (vocab, cols), 0) + 1
    lines = [low_ref[i : i + 1] for i in range(3)]
    lines += [tok_ref[i : i + 1] + 1 for i in range(rows)]
    lines += [high_ref[i : i + 1] for i in range(3)]
    framed = []
    for line in lines:
        hot = (ident == line).astype(F32).astype(BF16)
        framed.append(jnp.dot(table_ref[...], hot, preferred_element_type=F32))
    for r in range(rows):
        x_ref[r] = framed[r + 3].astype(BF16)

    def targets(r):
        return [(r // 2) * 2 * copies + 2 * k + r % 2 for k in range(copies)]

    scale = jnp.broadcast_to(scale_ref[...], (chans, cols))
    for r in range(rows):
        mixed = (grad_ref[r].astype(F32) * scale).astype(BF16)
        for d in targets(r):
            send_ref[d, 1] = mixed

    def emit(r, total):
        total = total.astype(BF16)
        for d in targets(r):
            send_ref[d, 0] = total

    conv_rows(framed, taps_ref, False, emit)


def join_kernel(near_ref, far_ref, out_ref):
    out_ref[0] = near_ref[...]
    out_ref[1] = far_ref[...]


def middle_kernel(
    own_ref, oth_ref, gain_ref, w0_ref, w1_ref, w2_ref,
    keep_ref, sib_ref,
    win, wout, scaled, gmix, normed, grads, act, gpre, sem,
):
    blocks, _, chans, cols = own_ref.shape
    width = blocks * chans
    hid = w0_ref.shape[1]
    shards = (w0_ref, w1_ref, w2_ref.at[0], w2_ref.at[1])
    pieces = [(ref.at[0], ref.at[1]) for ref in shards]
    copies = []
    for i, (a, b) in enumerate(pieces):
        spot = pl.ds(i * hid, hid)
        copies.append(pltpu.make_async_copy(a, win.at[spot], sem.at[2 * i]))
        copies.append(pltpu.make_async_copy(b, wout.at[spot], sem.at[2 * i + 1]))
    for copy in copies:
        copy.start()

    def cell(s, t):
        return jnp.concatenate([own_ref[s, t], oth_ref[s, t]], axis=1)

    zero = jnp.zeros((chans, 2 * cols), F32)
    total = lax.fori_loop(0, blocks, lambda s, acc: acc + cell(s, 0).astype(F32), zero, unroll=8)
    mean = jnp.sum(total, axis=0, keepdims=True) * (1.0 / width)

    def square(s, acc):
        diff = cell(s, 0).astype(F32) - mean
        return acc + diff * diff

    total = lax.fori_loop(0, blocks, square, zero, unroll=8)
    inv_std = lax.rsqrt(jnp.sum(total, axis=0, keepdims=True) * (1.0 / width) + 1e-06)

    def norm(s, carry):
        spot = pl.ds(pl.multiple_of(s * chans, chans), chans)
        value = (cell(s, 0).astype(F32) - mean) * inv_std
        gain = gain_ref[spot, :]
        normed[spot, :] = value
        scaled[spot, :] = (value * jnp.concatenate([gain, gain], axis=1)).astype(BF16)
        gmix[spot, :] = cell(s, 1)
        return carry

    lax.fori_loop(0, blocks, norm, 0, unroll=4)
    for copy in copies:
        copy.wait()

    for i in range(len(pieces)):
        spot = pl.ds(i * hid, hid)
        pre = jnp.dot(win[spot, :], scaled[...], preferred_element_type=F32)
        gact = jnp.dot(wout[spot, :], gmix[...], preferred_element_type=F32)
        cube = pre * pre
        tanh = jnp.tanh(ROOT * (pre + 0.044715 * (cube * pre)))
        half = 0.5 * (1.0 + tanh)
        act[spot, :] = (pre * half).astype(BF16)
        slope = half + (0.5 * pre) * (1.0 - tanh * tanh) * (ROOT * (1.0 + 0.134145 * cube))
        gpre[spot, :] = (gact * slope).astype(BF16)

    group = 256
    per = group // chans
    sums = [jnp.zeros((1, 2 * cols), F32), jnp.zeros((1, 2 * cols), F32)]
    turned = (((0,), (0,)), ((), ()))
    for j in range(width // group):
        spot = pl.ds(j * group, group)
        gain = gain_ref[spot, :]
        part = lax.dot_general(win[:, spot], gpre[...], turned, preferred_element_type=F32)
        part = part * jnp.concatenate([gain, gain], axis=1)
        grads[spot, :] = part
        sums[0] = sums[0] + jnp.sum(part, axis=0, keepdims=True)
        sums[1] = sums[1] + jnp.sum(part * normed[spot, :], axis=0, keepdims=True)
        mix = lax.dot_general(wout[:, spot], act[...], turned, preferred_element_type=F32)
        for q in range(per):
            piece = mix[q * chans : (q + 1) * chans]
            keep_ref[j * per + q, 0] = piece[:, :cols]
            sib_ref[j * per + q, 0] = piece[:, cols:].astype(BF16)
    first, second = sums[0] * (1.0 / width), sums[1] * (1.0 / width)

    def finish(s, carry):
        spot = pl.ds(pl.multiple_of(s * chans, chans), chans)
        piece = inv_std * (grads[spot, :] - first - normed[spot, :] * second)
        keep_ref[s, 1] = piece[:, :cols]
        sib_ref[s, 1] = piece[:, cols:].astype(BF16)
        return carry

    lax.fori_loop(0, blocks, finish, 0, unroll=4)


def sum_kernel(copies, got_ref, x_ref, scale_ref, out_ref, gconv_ref, low_ref, high_ref):
    rows, chans, cols = x_ref.shape
    scale = jnp.broadcast_to(scale_ref[...], (chans, cols))
    for r in range(rows):
        base = (r // 2) * 2 * copies + r % 2
        mix = got_ref[base, 0].astype(F32)
        conv = got_ref[base, 1].astype(F32)
        for k in range(1, copies):
            mix = mix + got_ref[base + 2 * k, 0].astype(F32)
            conv = conv + got_ref[base + 2 * k, 1].astype(F32)
        out_ref[r] = (x_ref[r].astype(F32) + scale * mix).astype(BF16)
        conv = conv.astype(BF16)
        gconv_ref[r] = conv
        if r < 3:
            low_ref[r] = conv
        if r >= rows - 3:
            high_ref[r - rows + 3] = conv


def last_kernel(gconv_ref, low_ref, high_ref, taps_ref, grad_ref, out_ref):
    rows = gconv_ref.shape[0]
    framed = [low_ref[i].astype(F32) for i in range(3)]
    framed += [gconv_ref[i].astype(F32) for i in range(rows)]
    framed += [high_ref[i].astype(F32) for i in range(3)]

    def emit(r, total):
        out_ref[r] = (grad_ref[r].astype(F32) + total).astype(BF16)

    conv_rows(framed, taps_ref, True, emit)


def call(body, outs, args, specs=None, scratch=(), flops=1 << 20, limit=32 << 20):
    outs = [jax.ShapeDtypeStruct(s, d) for s, d in outs]
    return pl.pallas_call(
        body,
        out_shape=outs,
        in_specs=specs or [VMEM] * len(args),
        out_specs=[VMEM] * len(outs),
        scratch_shapes=list(scratch),
        compiler_params=pltpu.CompilerParams(vmem_limit_bytes=limit),
        cost_estimate=pl.CostEstimate(flops=flops, bytes_accessed=4 << 20, transcendentals=0),
    )(*args)


def moved(shard, k):
    ny, nz, nx, nh, nc = (lax.axis_size(a) for a in AXES)

    def place(y, z, x, h, c):
        return (((y * nz + z) * nx + x) * nh + h) * nc + c

    pairs = []
    for y, z, x, h, c in itertools.product(*[range(n) for n in (ny, nz, nx, nh, nc)]):
        spot = (h * ny + y + turns(k, c)) % (ny * nh)
        other = (z, c) if z % 2 == c else (z ^ 1, 1 - c)
        pairs.append((place(spot % ny, other[0], x, spot // ny, other[1]), place(y, z, x, h, c)))
    return lax.ppermute(shard, AXES, pairs)


def turns(k, c):
    return (0, 1, -2 if c else 2, -1)[k]


def from_ring(shard, k):
    nh, ny = lax.axis_size("h"), lax.axis_size("y")
    ring = [y * nh + h for h in range(nh) for y in range(ny)]
    count = len(ring)
    pairs = [
        (ring[(i + turns(k, c)) % count] * 2 + c, ring[i] * 2 + c) for i in range(count) for c in range(2)
    ]
    return lax.ppermute(shard, ("y", "h", "c"), pairs)


def on_device(
    floor_tokens, token_table, depth_kernel, norm_gain, layer_scale, w_in, w_out, grad_out
):
    rows, cols = floor_tokens.shape
    chans = depth_kernel.shape[2]
    width = norm_gain.shape[0]
    blocks = width // chans
    copies = lax.axis_size("z") // 2
    hid = w_out.shape[0] * lax.axis_size("y")
    swap = [(0, 1), (1, 0)]

    both = jnp.stack([w_in.T, w_out])
    near, far = moved(both, 0), moved(both, 2)
    low, high = edges(floor_tokens[:3] + 1, floor_tokens[rows - 3 :] + 1)
    taps = depth_kernel.reshape(49, chans).T
    scale = lax.dynamic_slice_in_dim(layer_scale, lax.axis_index(CHAN) * chans, chans, 0)[:, None]
    gain = jnp.broadcast_to(norm_gain[:, None], (width, cols))
    grad_local = grad_out.transpose(0, 2, 1)

    tile = (rows, chans, cols)
    packed = (blocks, 2, chans, cols)
    x_local, send = call(
        functools.partial(first_kernel, copies),
        [(tile, BF16), (packed, BF16)],
        (floor_tokens, low, high, token_table.T, taps, scale, grad_local),
    )
    weights = [from_ring(near, 1), from_ring(near, 3)]
    own = lax.all_to_all(send, CHAN, 0, 0, tiled=True)
    (joined,) = call(join_kernel, [((2, 2, *w_out.shape), BF16)], (near, far), flops=20 << 30)
    own, joined = lax.optimization_barrier((own, joined))
    weights.append(joined)
    oth = lax.ppermute(own, "c", swap)
    keep, sib = call(
        middle_kernel,
        [(packed, F32), (packed, BF16)],
        (own, oth, gain, *weights),
        [VMEM] * 3 + [ANY] * 3,
        [
            pltpu.VMEM((hid, width), BF16),
            pltpu.VMEM((hid, width), BF16),
            pltpu.VMEM((width, 2 * cols), BF16),
            pltpu.VMEM((width, 2 * cols), BF16),
            pltpu.VMEM((width, 2 * cols), F32),
            pltpu.VMEM((width, 2 * cols), F32),
            pltpu.VMEM((hid, 2 * cols), BF16),
            pltpu.VMEM((hid, 2 * cols), BF16),
            pltpu.SemaphoreType.DMA((8,)),
        ],
        flops=8 * hid * width * 2 * cols,
        limit=40 << 20,
    )
    part = (keep + lax.ppermute(sib, "c", swap).astype(F32)).astype(BF16)
    got = lax.all_to_all(part, CHAN, 0, 0, tiled=True)
    edge = (3, chans, cols)
    block_out, gconv, low_side, high_side = call(
        functools.partial(sum_kernel, copies),
        [(tile, BF16), (tile, BF16), (edge, BF16), (edge, BF16)],
        (got, x_local, scale),
    )
    low, high = edges(low_side, high_side)
    (grad_embedded,) = call(last_kernel, [(tile, BF16)], (gconv, low, high, taps, grad_local))
    return block_out.transpose(0, 2, 1), grad_embedded.transpose(0, 2, 1)


def solution(mesh):
    chan, space = mesh.shape["chan"], mesh.shape["space"]
    grid = Mesh(mesh.devices.reshape(4, chan // 4, space // 4, 2, 2), AXES)
    placed = (
        P(SPACE, None),
        P(None, CHAN),
        P(None, None, CHAN),
        P(),
        P(),
        P(None, CHAN),
        P(CHAN, None),
        P(SPACE, None, CHAN),
    )
    return jax.shard_map(
        on_device,
        mesh=grid,
        in_specs=placed,
        out_specs=(P(SPACE, None, CHAN), P(SPACE, None, CHAN)),
        check_vma=False,
    )
```

```python
import functools
import itertools
import math

import jax
import jax.numpy as jnp
from jax import lax
from jax.experimental import pallas as pl
from jax.experimental.pallas import tpu as pltpu
from jax.sharding import Mesh, PartitionSpec as P

AXES = ("y", "z", "x", "h", "c")
CHAN = ("y", "z")
SPACE = ("x", "h", "c")
BF16, F32 = jnp.bfloat16, jnp.float32
VMEM = pl.BlockSpec(memory_space=pltpu.VMEM)
ANY = pl.BlockSpec(memory_space=pl.ANY)
ROOT = math.sqrt(2.0 / math.pi)


def edges(low_side, high_side):
    count = lax.axis_size(SPACE)
    forward = [(i, i + 1) for i in range(count - 1)]
    backward = [(j, i) for i, j in forward]
    return lax.ppermute(high_side, SPACE, forward), lax.ppermute(low_side, SPACE, backward)


def conv_rows(framed, taps_ref, flip, emit):
    rows = len(framed) - 6
    chans, cols = framed[0].shape
    lane = lax.broadcasted_iota(jnp.int32, (chans, cols), 1)
    totals = [jnp.zeros((chans, cols), F32) for _ in range(rows)]
    for b in range(7):
        step = (6 - b if flip else b) - 3
        taps = [
            jnp.broadcast_to(taps_ref[:, a * 7 + b : a * 7 + b + 1].astype(F32), (chans, cols))
            for a in range(7)
        ]
        inside = (lane + step >= 0) & (lane + step < cols)
        for i, tile in enumerate(framed):
            if step:
                tile = jnp.where(inside, pltpu.roll(tile, (-step) % cols, 1), 0.0)
            for a in range(7):
                r = i - (6 - a if flip else a)
                if 0 <= r < rows:
                    totals[r] = totals[r] + tile * taps[a]
    for r in range(rows):
        emit(r, totals[r])


def first_kernel(copies, tok_ref, low_ref, high_ref, table_ref, taps_ref, scale_ref, grad_ref, x_ref, send_ref):
    rows, cols = tok_ref.shape
    chans, vocab = table_ref.shape
    ident = lax.broadcasted_iota(jnp.int32, (vocab, cols), 0) + 1
    lines = [low_ref[i : i + 1] for i in range(3)]
    lines += [tok_ref[i : i + 1] + 1 for i in range(rows)]
    lines += [high_ref[i : i + 1] for i in range(3)]
    framed = []
    for line in lines:
        hot = (ident == line).astype(F32).astype(BF16)
        framed.append(jnp.dot(table_ref[...], hot, preferred_element_type=F32))
    for r in range(rows):
        x_ref[r] = framed[r + 3].astype(BF16)

    def targets(r):
        return [(r // 2) * 2 * copies + 2 * k + r % 2 for k in range(copies)]

    scale = jnp.broadcast_to(scale_ref[...], (chans, cols))
    for r in range(rows):
        mixed = (grad_ref[r].astype(F32) * scale).astype(BF16)
        for d in targets(r):
            send_ref[d, 1] = mixed

    def emit(r, total):
        total = total.astype(BF16)
        for d in targets(r):
            send_ref[d, 0] = total

    conv_rows(framed, taps_ref, False, emit)


def stack_kernel(in_ref, out_ref, both_ref):
    both_ref[0] = in_ref[...].T
    both_ref[1] = out_ref[...]


def join_kernel(near_ref, far_ref, out_ref):
    out_ref[0] = near_ref[...]
    out_ref[1] = far_ref[...]


def middle_kernel(
    own_ref, oth_ref, gain_ref, w0_ref, w1_ref, w2_ref,
    keep_ref, sib_ref,
    win, wout, scaled, gmix, normed, grads, act, gpre, sem,
):
    blocks, _, chans, cols = own_ref.shape
    width = blocks * chans
    hid = w0_ref.shape[1]
    shards = (w0_ref, w1_ref, w2_ref.at[0], w2_ref.at[1])
    pieces = [(ref.at[0], ref.at[1]) for ref in shards]
    copies = []
    for i, (a, b) in enumerate(pieces):
        spot = pl.ds(i * hid, hid)
        copies.append(pltpu.make_async_copy(a, win.at[spot], sem.at[2 * i]))
        copies.append(pltpu.make_async_copy(b, wout.at[spot], sem.at[2 * i + 1]))
    for copy in copies:
        copy.start()

    def cell(s, t):
        return jnp.concatenate([own_ref[s, t], oth_ref[s, t]], axis=1)

    zero = jnp.zeros((chans, 2 * cols), F32)
    total = lax.fori_loop(0, blocks, lambda s, acc: acc + cell(s, 0).astype(F32), zero, unroll=8)
    mean = jnp.sum(total, axis=0, keepdims=True) * (1.0 / width)

    def square(s, acc):
        diff = cell(s, 0).astype(F32) - mean
        return acc + diff * diff

    total = lax.fori_loop(0, blocks, square, zero, unroll=8)
    inv_std = lax.rsqrt(jnp.sum(total, axis=0, keepdims=True) * (1.0 / width) + 1e-06)

    def norm(s, carry):
        spot = pl.ds(pl.multiple_of(s * chans, chans), chans)
        value = (cell(s, 0).astype(F32) - mean) * inv_std
        gain = gain_ref[spot, :]
        normed[spot, :] = value
        scaled[spot, :] = (value * jnp.concatenate([gain, gain], axis=1)).astype(BF16)
        gmix[spot, :] = cell(s, 1)
        return carry

    lax.fori_loop(0, blocks, norm, 0, unroll=4)
    for copy in copies:
        copy.wait()

    for i in range(len(pieces)):
        spot = pl.ds(i * hid, hid)
        pre = jnp.dot(win[spot, :], scaled[...], preferred_element_type=F32)
        gact = jnp.dot(wout[spot, :], gmix[...], preferred_element_type=F32)
        cube = pre * pre
        tanh = jnp.tanh(ROOT * (pre + 0.044715 * (cube * pre)))
        half = 0.5 * (1.0 + tanh)
        act[spot, :] = (pre * half).astype(BF16)
        slope = half + (0.5 * pre) * (1.0 - tanh * tanh) * (ROOT * (1.0 + 0.134145 * cube))
        gpre[spot, :] = (gact * slope).astype(BF16)

    group = 256
    per = group // chans
    sums = [jnp.zeros((1, 2 * cols), F32), jnp.zeros((1, 2 * cols), F32)]
    turned = (((0,), (0,)), ((), ()))
    for j in range(width // group):
        spot = pl.ds(j * group, group)
        gain = gain_ref[spot, :]
        part = lax.dot_general(win[:, spot], gpre[...], turned, preferred_element_type=F32)
        part = part * jnp.concatenate([gain, gain], axis=1)
        grads[spot, :] = part
        sums[0] = sums[0] + jnp.sum(part, axis=0, keepdims=True)
        sums[1] = sums[1] + jnp.sum(part * normed[spot, :], axis=0, keepdims=True)
        mix = lax.dot_general(wout[:, spot], act[...], turned, preferred_element_type=F32)
        for q in range(per):
            piece = mix[q * chans : (q + 1) * chans]
            keep_ref[j * per + q, 0] = piece[:, :cols]
            sib_ref[j * per + q, 0] = piece[:, cols:].astype(BF16)
    first, second = sums[0] * (1.0 / width), sums[1] * (1.0 / width)

    def finish(s, carry):
        spot = pl.ds(pl.multiple_of(s * chans, chans), chans)
        piece = inv_std * (grads[spot, :] - first - normed[spot, :] * second)
        keep_ref[s, 1] = piece[:, :cols]
        sib_ref[s, 1] = piece[:, cols:].astype(BF16)
        return carry

    lax.fori_loop(0, blocks, finish, 0, unroll=4)


def sum_kernel(copies, got_ref, x_ref, scale_ref, out_ref, gconv_ref, low_ref, high_ref):
    rows, chans, cols = x_ref.shape
    scale = jnp.broadcast_to(scale_ref[...], (chans, cols))
    for r in range(rows):
        base = (r // 2) * 2 * copies + r % 2
        mix = got_ref[base, 0].astype(F32)
        conv = got_ref[base, 1].astype(F32)
        for k in range(1, copies):
            mix = mix + got_ref[base + 2 * k, 0].astype(F32)
            conv = conv + got_ref[base + 2 * k, 1].astype(F32)
        out_ref[r] = (x_ref[r].astype(F32) + scale * mix).astype(BF16)
        conv = conv.astype(BF16)
        gconv_ref[r] = conv
        if r < 3:
            low_ref[r] = conv
        if r >= rows - 3:
            high_ref[r - rows + 3] = conv


def last_kernel(gconv_ref, low_ref, high_ref, taps_ref, grad_ref, out_ref):
    rows = gconv_ref.shape[0]
    framed = [low_ref[i].astype(F32) for i in range(3)]
    framed += [gconv_ref[i].astype(F32) for i in range(rows)]
    framed += [high_ref[i].astype(F32) for i in range(3)]

    def emit(r, total):
        out_ref[r] = (grad_ref[r].astype(F32) + total).astype(BF16)

    conv_rows(framed, taps_ref, True, emit)


def call(body, outs, args, specs=None, scratch=(), flops=1 << 20, limit=32 << 20):
    outs = [jax.ShapeDtypeStruct(s, d) for s, d in outs]
    return pl.pallas_call(
        body,
        out_shape=outs,
        in_specs=specs or [VMEM] * len(args),
        out_specs=[VMEM] * len(outs),
        scratch_shapes=list(scratch),
        compiler_params=pltpu.CompilerParams(vmem_limit_bytes=limit),
        cost_estimate=pl.CostEstimate(flops=flops, bytes_accessed=4 << 20, transcendentals=0),
    )(*args)


def moved(shard, k):
    ny, nz, nx, nh, nc = (lax.axis_size(a) for a in AXES)

    def place(y, z, x, h, c):
        return (((y * nz + z) * nx + x) * nh + h) * nc + c

    pairs = []
    for y, z, x, h, c in itertools.product(*[range(n) for n in (ny, nz, nx, nh, nc)]):
        spot = (h * ny + y + turns(k, c)) % (ny * nh)
        other = (z, c) if z % 2 == c else (z ^ 1, 1 - c)
        pairs.append((place(spot % ny, other[0], x, spot // ny, other[1]), place(y, z, x, h, c)))
    return lax.ppermute(shard, AXES, pairs)


def turns(k, c):
    return (0, 1, -2 if c else 2, -1)[k]


def from_ring(shard, k):
    nh, ny = lax.axis_size("h"), lax.axis_size("y")
    ring = [y * nh + h for h in range(nh) for y in range(ny)]
    count = len(ring)
    pairs = [
        (ring[(i + turns(k, c)) % count] * 2 + c, ring[i] * 2 + c) for i in range(count) for c in range(2)
    ]
    return lax.ppermute(shard, ("y", "h", "c"), pairs)


def on_device(
    floor_tokens, token_table, depth_kernel, norm_gain, layer_scale, w_in, w_out, grad_out
):
    rows, cols = floor_tokens.shape
    chans = depth_kernel.shape[2]
    width = norm_gain.shape[0]
    blocks = width // chans
    copies = lax.axis_size("z") // 2
    hid = w_out.shape[0] * lax.axis_size("y")
    swap = [(0, 1), (1, 0)]

    (both,) = call(stack_kernel, [((2, *w_out.shape), BF16)], (w_in, w_out))
    near, far = moved(both, 0), moved(both, 2)
    low, high = edges(floor_tokens[:3] + 1, floor_tokens[rows - 3 :] + 1)
    taps = depth_kernel.reshape(49, chans).T
    scale = lax.dynamic_slice_in_dim(layer_scale, lax.axis_index(CHAN) * chans, chans, 0)[:, None]
    gain = jnp.broadcast_to(norm_gain[:, None], (width, cols))
    grad_local = grad_out.transpose(0, 2, 1)

    tile = (rows, chans, cols)
    packed = (blocks, 2, chans, cols)
    x_local, send = call(
        functools.partial(first_kernel, copies),
        [(tile, BF16), (packed, BF16)],
        (floor_tokens, low, high, token_table.T, taps, scale, grad_local),
    )
    weights = [from_ring(near, 1), from_ring(near, 3)]
    own = lax.all_to_all(send, CHAN, 0, 0, tiled=True)
    (joined,) = call(join_kernel, [((2, 2, *w_out.shape), BF16)], (near, far), flops=20 << 30)
    own, joined = lax.optimization_barrier((own, joined))
    weights.append(joined)
    oth = lax.ppermute(own, "c", swap)
    keep, sib = call(
        middle_kernel,
        [(packed, F32), (packed, BF16)],
        (own, oth, gain, *weights),
        [VMEM] * 3 + [ANY] * 3,
        [
            pltpu.VMEM((hid, width), BF16),
            pltpu.VMEM((hid, width), BF16),
            pltpu.VMEM((width, 2 * cols), BF16),
            pltpu.VMEM((width, 2 * cols), BF16),
            pltpu.VMEM((width, 2 * cols), F32),
            pltpu.VMEM((width, 2 * cols), F32),
            pltpu.VMEM((hid, 2 * cols), BF16),
            pltpu.VMEM((hid, 2 * cols), BF16),
            pltpu.SemaphoreType.DMA((8,)),
        ],
        flops=8 * hid * width * 2 * cols,
        limit=40 << 20,
    )
    part = (keep + lax.ppermute(sib, "c", swap).astype(F32)).astype(BF16)
    got = lax.all_to_all(part, CHAN, 0, 0, tiled=True)
    edge = (3, chans, cols)
    block_out, gconv, low_side, high_side = call(
        functools.partial(sum_kernel, copies),
        [(tile, BF16), (tile, BF16), (edge, BF16), (edge, BF16)],
        (got, x_local, scale),
    )
    low, high = edges(low_side, high_side)
    (grad_embedded,) = call(last_kernel, [(tile, BF16)], (gconv, low, high, taps, grad_local))
    return block_out.transpose(0, 2, 1), grad_embedded.transpose(0, 2, 1)


def solution(mesh):
    chan, space = mesh.shape["chan"], mesh.shape["space"]
    grid = Mesh(mesh.devices.reshape(4, chan // 4, space // 4, 2, 2), AXES)
    placed = (
        P(SPACE, None),
        P(None, CHAN),
        P(None, None, CHAN),
        P(),
        P(),
        P(None, CHAN),
        P(CHAN, None),
        P(SPACE, None, CHAN),
    )
    return jax.shard_map(
        on_device,
        mesh=grid,
        in_specs=placed,
        out_specs=(P(SPACE, None, CHAN), P(SPACE, None, CHAN)),
        check_vma=False,
    )
```

```python
import functools
import itertools
import math

import jax
import jax.numpy as jnp
from jax import lax
from jax.experimental import pallas as pl
from jax.experimental.pallas import tpu as pltpu
from jax.sharding import Mesh, PartitionSpec as P

AXES = ("y", "z", "x", "h", "c")
CHAN = ("y", "z")
SPACE = ("x", "h", "c")
BF16, F32 = jnp.bfloat16, jnp.float32
VMEM = pl.BlockSpec(memory_space=pltpu.VMEM)
ANY = pl.BlockSpec(memory_space=pl.ANY)
ROOT = math.sqrt(2.0 / math.pi)


def edges(low_side, high_side):
    count = lax.axis_size(SPACE)
    forward = [(i, i + 1) for i in range(count - 1)]
    backward = [(j, i) for i, j in forward]
    return lax.ppermute(high_side, SPACE, forward), lax.ppermute(low_side, SPACE, backward)


def conv_rows(framed, taps_ref, flip, emit):
    rows = len(framed) - 6
    chans, cols = framed[0].shape
    lane = lax.broadcasted_iota(jnp.int32, (chans, cols), 1)
    totals = [jnp.zeros((chans, cols), F32) for _ in range(rows)]
    for b in range(7):
        step = (6 - b if flip else b) - 3
        taps = [
            jnp.broadcast_to(taps_ref[:, a * 7 + b : a * 7 + b + 1].astype(F32), (chans, cols))
            for a in range(7)
        ]
        inside = (lane + step >= 0) & (lane + step < cols)
        for i, tile in enumerate(framed):
            if step:
                tile = jnp.where(inside, pltpu.roll(tile, (-step) % cols, 1), 0.0)
            for a in range(7):
                r = i - (6 - a if flip else a)
                if 0 <= r < rows:
                    totals[r] = totals[r] + tile * taps[a]
    for r in range(rows):
        emit(r, totals[r])


def first_kernel(copies, tok_ref, low_ref, high_ref, table_ref, taps_ref, scale_ref, grad_ref, x_ref, send_ref):
    rows, cols = tok_ref.shape
    chans, vocab = table_ref.shape
    ident = lax.broadcasted_iota(jnp.int32, (vocab, cols), 0) + 1
    lines = [low_ref[i : i + 1] for i in range(3)]
    lines += [tok_ref[i : i + 1] + 1 for i in range(rows)]
    lines += [high_ref[i : i + 1] for i in range(3)]
    framed = []
    for line in lines:
        hot = (ident == line).astype(F32).astype(BF16)
        framed.append(jnp.dot(table_ref[...], hot, preferred_element_type=F32))
    for r in range(rows):
        x_ref[r] = framed[r + 3].astype(BF16)

    def targets(r):
        return [(r // 2) * 2 * copies + 2 * k + r % 2 for k in range(copies)]

    scale = jnp.broadcast_to(scale_ref[...], (chans, cols))
    for r in range(rows):
        mixed = (grad_ref[r].astype(F32) * scale).astype(BF16)
        for d in targets(r):
            send_ref[d, 1] = mixed

    def emit(r, total):
        total = total.astype(BF16)
        for d in targets(r):
            send_ref[d, 0] = total

    conv_rows(framed, taps_ref, False, emit)


def stack_kernel(in_ref, out_ref, both_ref):
    both_ref[0] = in_ref[...].T
    both_ref[1] = out_ref[...]


def anchor_kernel(near_ref, far_ref, out_ref):
    out_ref[...] = near_ref[0, :16, :128] + far_ref[0, :16, :128]


def middle_kernel(
    own_ref, oth_ref, gain_ref, w0_ref, w1_ref, w2_ref, w3_ref, _,
    keep_ref, sib_ref,
    win, wout, scaled, gmix, normed, grads, act, gpre, sem,
):
    blocks, _, chans, cols = own_ref.shape
    width = blocks * chans
    hid = w0_ref.shape[1]
    pieces = [(ref.at[0], ref.at[1]) for ref in (w0_ref, w1_ref, w2_ref, w3_ref)]
    copies = []
    for i, (a, b) in enumerate(pieces):
        spot = pl.ds(i * hid, hid)
        copies.append(pltpu.make_async_copy(a, win.at[spot], sem.at[2 * i]))
        copies.append(pltpu.make_async_copy(b, wout.at[spot], sem.at[2 * i + 1]))
    for copy in copies:
        copy.start()

    def cell(s, t):
        return jnp.concatenate([own_ref[s, t], oth_ref[s, t]], axis=1)

    zero = jnp.zeros((chans, 2 * cols), F32)
    total = lax.fori_loop(0, blocks, lambda s, acc: acc + cell(s, 0).astype(F32), zero, unroll=8)
    mean = jnp.sum(total, axis=0, keepdims=True) * (1.0 / width)

    def square(s, acc):
        diff = cell(s, 0).astype(F32) - mean
        return acc + diff * diff

    total = lax.fori_loop(0, blocks, square, zero, unroll=8)
    inv_std = lax.rsqrt(jnp.sum(total, axis=0, keepdims=True) * (1.0 / width) + 1e-06)

    def norm(s, carry):
        spot = pl.ds(pl.multiple_of(s * chans, chans), chans)
        value = (cell(s, 0).astype(F32) - mean) * inv_std
        gain = gain_ref[spot, :]
        normed[spot, :] = value
        scaled[spot, :] = (value * jnp.concatenate([gain, gain], axis=1)).astype(BF16)
        gmix[spot, :] = cell(s, 1)
        return carry

    lax.fori_loop(0, blocks, norm, 0, unroll=4)
    for copy in copies:
        copy.wait()

    for i in range(len(pieces)):
        spot = pl.ds(i * hid, hid)
        pre = jnp.dot(win[spot, :], scaled[...], preferred_element_type=F32)
        gact = jnp.dot(wout[spot, :], gmix[...], preferred_element_type=F32)
        cube = pre * pre
        tanh = jnp.tanh(ROOT * (pre + 0.044715 * (cube * pre)))
        half = 0.5 * (1.0 + tanh)
        act[spot, :] = (pre * half).astype(BF16)
        slope = half + (0.5 * pre) * (1.0 - tanh * tanh) * (ROOT * (1.0 + 0.134145 * cube))
        gpre[spot, :] = (gact * slope).astype(BF16)

    group = 256
    per = group // chans
    sums = [jnp.zeros((1, 2 * cols), F32), jnp.zeros((1, 2 * cols), F32)]
    turned = (((0,), (0,)), ((), ()))
    for j in range(width // group):
        spot = pl.ds(j * group, group)
        gain = gain_ref[spot, :]
        part = lax.dot_general(win[:, spot], gpre[...], turned, preferred_element_type=F32)
        part = part * jnp.concatenate([gain, gain], axis=1)
        grads[spot, :] = part
        sums[0] = sums[0] + jnp.sum(part, axis=0, keepdims=True)
        sums[1] = sums[1] + jnp.sum(part * normed[spot, :], axis=0, keepdims=True)
        mix = lax.dot_general(wout[:, spot], act[...], turned, preferred_element_type=F32)
        for q in range(per):
            piece = mix[q * chans : (q + 1) * chans]
            keep_ref[j * per + q, 0] = piece[:, :cols]
            sib_ref[j * per + q, 0] = piece[:, cols:].astype(BF16)
    first, second = sums[0] * (1.0 / width), sums[1] * (1.0 / width)

    def finish(s, carry):
        spot = pl.ds(pl.multiple_of(s * chans, chans), chans)
        piece = inv_std * (grads[spot, :] - first - normed[spot, :] * second)
        keep_ref[s, 1] = piece[:, :cols]
        sib_ref[s, 1] = piece[:, cols:].astype(BF16)
        return carry

    lax.fori_loop(0, blocks, finish, 0, unroll=4)


def sum_kernel(copies, got_ref, x_ref, scale_ref, out_ref, gconv_ref, low_ref, high_ref):
    rows, chans, cols = x_ref.shape
    scale = jnp.broadcast_to(scale_ref[...], (chans, cols))
    for r in range(rows):
        base = (r // 2) * 2 * copies + r % 2
        mix = got_ref[base, 0].astype(F32)
        conv = got_ref[base, 1].astype(F32)
        for k in range(1, copies):
            mix = mix + got_ref[base + 2 * k, 0].astype(F32)
            conv = conv + got_ref[base + 2 * k, 1].astype(F32)
        out_ref[r] = (x_ref[r].astype(F32) + scale * mix).astype(BF16)
        conv = conv.astype(BF16)
        gconv_ref[r] = conv
        if r < 3:
            low_ref[r] = conv
        if r >= rows - 3:
            high_ref[r - rows + 3] = conv


def last_kernel(gconv_ref, low_ref, high_ref, taps_ref, grad_ref, out_ref):
    rows = gconv_ref.shape[0]
    framed = [low_ref[i].astype(F32) for i in range(3)]
    framed += [gconv_ref[i].astype(F32) for i in range(rows)]
    framed += [high_ref[i].astype(F32) for i in range(3)]

    def emit(r, total):
        out_ref[r] = (grad_ref[r].astype(F32) + total).astype(BF16)

    conv_rows(framed, taps_ref, True, emit)


def call(body, outs, args, specs=None, scratch=(), flops=1 << 20, limit=32 << 20):
    outs = [jax.ShapeDtypeStruct(s, d) for s, d in outs]
    return pl.pallas_call(
        body,
        out_shape=outs,
        in_specs=specs or [VMEM] * len(args),
        out_specs=[VMEM] * len(outs),
        scratch_shapes=list(scratch),
        compiler_params=pltpu.CompilerParams(vmem_limit_bytes=limit),
        cost_estimate=pl.CostEstimate(flops=flops, bytes_accessed=4 << 20, transcendentals=0),
    )(*args)


def moved(shard, k):
    ny, nz, nx, nh, nc = (lax.axis_size(a) for a in AXES)

    def place(y, z, x, h, c):
        return (((y * nz + z) * nx + x) * nh + h) * nc + c

    pairs = []
    for y, z, x, h, c in itertools.product(*[range(n) for n in (ny, nz, nx, nh, nc)]):
        spot = (h * ny + y + turns(k, c)) % (ny * nh)
        other = (z, c) if z % 2 == c else (z ^ 1, 1 - c)
        pairs.append((place(spot % ny, other[0], x, spot // ny, other[1]), place(y, z, x, h, c)))
    return lax.ppermute(shard, AXES, pairs)


def turns(k, c):
    return (0, 1, -2 if c else 2, -1)[k]


def from_ring(shard, k):
    nh, ny = lax.axis_size("h"), lax.axis_size("y")
    ring = [y * nh + h for h in range(nh) for y in range(ny)]
    count = len(ring)
    pairs = [
        (ring[(i + turns(k, c)) % count] * 2 + c, ring[i] * 2 + c) for i in range(count) for c in range(2)
    ]
    return lax.ppermute(shard, ("y", "h", "c"), pairs)


def on_device(
    floor_tokens, token_table, depth_kernel, norm_gain, layer_scale, w_in, w_out, grad_out
):
    rows, cols = floor_tokens.shape
    chans = depth_kernel.shape[2]
    width = norm_gain.shape[0]
    blocks = width // chans
    copies = lax.axis_size("z") // 2
    hid = w_out.shape[0] * lax.axis_size("y")
    swap = [(0, 1), (1, 0)]

    (both,) = call(stack_kernel, [((2, *w_out.shape), BF16)], (w_in, w_out))
    near, far = moved(both, 0), moved(both, 2)
    low, high = edges(floor_tokens[:3] + 1, floor_tokens[rows - 3 :] + 1)
    taps = depth_kernel.reshape(49, chans).T
    scale = lax.dynamic_slice_in_dim(layer_scale, lax.axis_index(CHAN) * chans, chans, 0)[:, None]
    gain = jnp.broadcast_to(norm_gain[:, None], (width, cols))
    grad_local = grad_out.transpose(0, 2, 1)

    tile = (rows, chans, cols)
    packed = (blocks, 2, chans, cols)
    x_local, send = call(
        functools.partial(first_kernel, copies),
        [(tile, BF16), (packed, BF16)],
        (floor_tokens, low, high, token_table.T, taps, scale, grad_local),
    )
    weights = [from_ring(near, 1), from_ring(near, 3)]
    own = lax.all_to_all(send, CHAN, 0, 0, tiled=True)
    (anchor,) = call(anchor_kernel, [((16, 128), BF16)], (near, far), flops=20 << 30)
    own, anchor = lax.optimization_barrier((own, anchor))
    weights += [near, far, anchor]
    oth = lax.ppermute(own, "c", swap)
    keep, sib = call(
        middle_kernel,
        [(packed, F32), (packed, BF16)],
        (own, oth, gain, *weights),
        [VMEM] * 3 + [ANY] * 5,
        [
            pltpu.VMEM((hid, width), BF16),
            pltpu.VMEM((hid, width), BF16),
            pltpu.VMEM((width, 2 * cols), BF16),
            pltpu.VMEM((width, 2 * cols), BF16),
            pltpu.VMEM((width, 2 * cols), F32),
            pltpu.VMEM((width, 2 * cols), F32),
            pltpu.VMEM((hid, 2 * cols), BF16),
            pltpu.VMEM((hid, 2 * cols), BF16),
            pltpu.SemaphoreType.DMA((8,)),
        ],
        flops=8 * hid * width * 2 * cols,
        limit=40 << 20,
    )
    part = (keep + lax.ppermute(sib, "c", swap).astype(F32)).astype(BF16)
    got = lax.all_to_all(part, CHAN, 0, 0, tiled=True)
    edge = (3, chans, cols)
    block_out, gconv, low_side, high_side = call(
        functools.partial(sum_kernel, copies),
        [(tile, BF16), (tile, BF16), (edge, BF16), (edge, BF16)],
        (got, x_local, scale),
    )
    low, high = edges(low_side, high_side)
    (grad_embedded,) = call(last_kernel, [(tile, BF16)], (gconv, low, high, taps, grad_local))
    return block_out.transpose(0, 2, 1), grad_embedded.transpose(0, 2, 1)


def solution(mesh):
    chan, space = mesh.shape["chan"], mesh.shape["space"]
    grid = Mesh(mesh.devices.reshape(4, chan // 4, space // 4, 2, 2), AXES)
    placed = (
        P(SPACE, None),
        P(None, CHAN),
        P(None, None, CHAN),
        P(),
        P(),
        P(None, CHAN),
        P(CHAN, None),
        P(SPACE, None, CHAN),
    )
    return jax.shard_map(
        on_device,
        mesh=grid,
        in_specs=placed,
        out_specs=(P(SPACE, None, CHAN), P(SPACE, None, CHAN)),
        check_vma=False,
    )
```

```python
import functools
import itertools
import math

import jax
import jax.numpy as jnp
from jax import lax
from jax.experimental import pallas as pl
from jax.experimental.pallas import tpu as pltpu
from jax.sharding import Mesh, PartitionSpec as P

AXES = ("y", "z", "x", "h", "c")
CHAN = ("y", "z")
SPACE = ("x", "h", "c")
BF16, F32 = jnp.bfloat16, jnp.float32
VMEM = pl.BlockSpec(memory_space=pltpu.VMEM)
ANY = pl.BlockSpec(memory_space=pl.ANY)
ROOT = math.sqrt(2.0 / math.pi)


def edges(low_side, high_side):
    count = lax.axis_size(SPACE)
    forward = [(i, i + 1) for i in range(count - 1)]
    backward = [(j, i) for i, j in forward]
    return lax.ppermute(high_side, SPACE, forward), lax.ppermute(low_side, SPACE, backward)


def conv_rows(framed, taps_ref, flip, emit):
    rows = len(framed) - 6
    chans, cols = framed[0].shape
    lane = lax.broadcasted_iota(jnp.int32, (chans, cols), 1)
    totals = [jnp.zeros((chans, cols), F32) for _ in range(rows)]
    for b in range(7):
        step = (6 - b if flip else b) - 3
        taps = [
            jnp.broadcast_to(taps_ref[:, a * 7 + b : a * 7 + b + 1].astype(F32), (chans, cols))
            for a in range(7)
        ]
        inside = (lane + step >= 0) & (lane + step < cols)
        for i, tile in enumerate(framed):
            if step:
                tile = jnp.where(inside, pltpu.roll(tile, (-step) % cols, 1), 0.0)
            for a in range(7):
                r = i - (6 - a if flip else a)
                if 0 <= r < rows:
                    totals[r] = totals[r] + tile * taps[a]
    for r in range(rows):
        emit(r, totals[r])


def first_kernel(copies, tok_ref, low_ref, high_ref, table_ref, taps_ref, scale_ref, grad_ref, x_ref, send_ref):
    rows, cols = tok_ref.shape
    chans, vocab = table_ref.shape
    ident = lax.broadcasted_iota(jnp.int32, (vocab, cols), 0) + 1
    lines = [low_ref[i : i + 1] for i in range(3)]
    lines += [tok_ref[i : i + 1] + 1 for i in range(rows)]
    lines += [high_ref[i : i + 1] for i in range(3)]
    framed = []
    for line in lines:
        hot = (ident == line).astype(F32).astype(BF16)
        framed.append(jnp.dot(table_ref[...], hot, preferred_element_type=F32))
    for r in range(rows):
        x_ref[r] = framed[r + 3].astype(BF16)

    def targets(r):
        return [(r // 2) * 2 * copies + 2 * k + r % 2 for k in range(copies)]

    scale = jnp.broadcast_to(scale_ref[...], (chans, cols))
    for r in range(rows):
        mixed = (grad_ref[r].astype(F32) * scale).astype(BF16)
        for d in targets(r):
            send_ref[d, 1] = mixed

    def emit(r, total):
        total = total.astype(BF16)
        for d in targets(r):
            send_ref[d, 0] = total

    conv_rows(framed, taps_ref, False, emit)


def stack_kernel(in_ref, out_ref, both_ref, shard, sem):
    first = pltpu.make_async_copy(in_ref, shard, sem.at[0])
    second = pltpu.make_async_copy(out_ref, both_ref.at[1], sem.at[1])
    first.start()
    second.start()
    first.wait()
    both_ref[0] = shard[...].T
    second.wait()


def anchor_kernel(near_ref, far_ref, out_ref):
    out_ref[...] = near_ref[0, :16, :128] + far_ref[0, :16, :128]


def middle_kernel(
    own_ref, oth_ref, gain_ref, w0_ref, w1_ref, w2_ref, w3_ref, _,
    keep_ref, sib_ref,
    win, wout, scaled, gmix, normed, grads, act, gpre, sem,
):
    blocks, _, chans, cols = own_ref.shape
    width = blocks * chans
    hid = w0_ref.shape[1]
    pieces = [(ref.at[0], ref.at[1]) for ref in (w0_ref, w1_ref, w2_ref, w3_ref)]
    copies = []
    for i, (a, b) in enumerate(pieces):
        spot = pl.ds(i * hid, hid)
        copies.append(pltpu.make_async_copy(a, win.at[spot], sem.at[2 * i]))
        copies.append(pltpu.make_async_copy(b, wout.at[spot], sem.at[2 * i + 1]))
    for copy in copies:
        copy.start()

    def cell(s, t):
        return jnp.concatenate([own_ref[s, t], oth_ref[s, t]], axis=1)

    zero = jnp.zeros((chans, 2 * cols), F32)
    total = lax.fori_loop(0, blocks, lambda s, acc: acc + cell(s, 0).astype(F32), zero, unroll=8)
    mean = jnp.sum(total, axis=0, keepdims=True) * (1.0 / width)

    def square(s, acc):
        diff = cell(s, 0).astype(F32) - mean
        return acc + diff * diff

    total = lax.fori_loop(0, blocks, square, zero, unroll=8)
    inv_std = lax.rsqrt(jnp.sum(total, axis=0, keepdims=True) * (1.0 / width) + 1e-06)

    def norm(s, carry):
        spot = pl.ds(pl.multiple_of(s * chans, chans), chans)
        value = (cell(s, 0).astype(F32) - mean) * inv_std
        gain = gain_ref[spot, :]
        normed[spot, :] = value
        scaled[spot, :] = (value * jnp.concatenate([gain, gain], axis=1)).astype(BF16)
        gmix[spot, :] = cell(s, 1)
        return carry

    lax.fori_loop(0, blocks, norm, 0, unroll=4)
    for copy in copies:
        copy.wait()

    for i in range(len(pieces)):
        spot = pl.ds(i * hid, hid)
        pre = jnp.dot(win[spot, :], scaled[...], preferred_element_type=F32)
        gact = jnp.dot(wout[spot, :], gmix[...], preferred_element_type=F32)
        cube = pre * pre
        tanh = jnp.tanh(ROOT * (pre + 0.044715 * (cube * pre)))
        half = 0.5 * (1.0 + tanh)
        act[spot, :] = (pre * half).astype(BF16)
        slope = half + (0.5 * pre) * (1.0 - tanh * tanh) * (ROOT * (1.0 + 0.134145 * cube))
        gpre[spot, :] = (gact * slope).astype(BF16)

    group = 256
    per = group // chans
    sums = [jnp.zeros((1, 2 * cols), F32), jnp.zeros((1, 2 * cols), F32)]
    turned = (((0,), (0,)), ((), ()))
    for j in range(width // group):
        spot = pl.ds(j * group, group)
        gain = gain_ref[spot, :]
        part = lax.dot_general(win[:, spot], gpre[...], turned, preferred_element_type=F32)
        part = part * jnp.concatenate([gain, gain], axis=1)
        grads[spot, :] = part
        sums[0] = sums[0] + jnp.sum(part, axis=0, keepdims=True)
        sums[1] = sums[1] + jnp.sum(part * normed[spot, :], axis=0, keepdims=True)
        mix = lax.dot_general(wout[:, spot], act[...], turned, preferred_element_type=F32)
        for q in range(per):
            piece = mix[q * chans : (q + 1) * chans]
            keep_ref[j * per + q, 0] = piece[:, :cols]
            sib_ref[j * per + q, 0] = piece[:, cols:].astype(BF16)
    first, second = sums[0] * (1.0 / width), sums[1] * (1.0 / width)

    def finish(s, carry):
        spot = pl.ds(pl.multiple_of(s * chans, chans), chans)
        piece = inv_std * (grads[spot, :] - first - normed[spot, :] * second)
        keep_ref[s, 1] = piece[:, :cols]
        sib_ref[s, 1] = piece[:, cols:].astype(BF16)
        return carry

    lax.fori_loop(0, blocks, finish, 0, unroll=4)


def sum_kernel(copies, got_ref, x_ref, scale_ref, out_ref, gconv_ref, low_ref, high_ref):
    rows, chans, cols = x_ref.shape
    scale = jnp.broadcast_to(scale_ref[...], (chans, cols))
    for r in range(rows):
        base = (r // 2) * 2 * copies + r % 2
        mix = got_ref[base, 0].astype(F32)
        conv = got_ref[base, 1].astype(F32)
        for k in range(1, copies):
            mix = mix + got_ref[base + 2 * k, 0].astype(F32)
            conv = conv + got_ref[base + 2 * k, 1].astype(F32)
        out_ref[r] = (x_ref[r].astype(F32) + scale * mix).astype(BF16)
        conv = conv.astype(BF16)
        gconv_ref[r] = conv
        if r < 3:
            low_ref[r] = conv
        if r >= rows - 3:
            high_ref[r - rows + 3] = conv


def last_kernel(gconv_ref, low_ref, high_ref, taps_ref, grad_ref, out_ref):
    rows = gconv_ref.shape[0]
    framed = [low_ref[i].astype(F32) for i in range(3)]
    framed += [gconv_ref[i].astype(F32) for i in range(rows)]
    framed += [high_ref[i].astype(F32) for i in range(3)]

    def emit(r, total):
        out_ref[r] = (grad_ref[r].astype(F32) + total).astype(BF16)

    conv_rows(framed, taps_ref, True, emit)


def call(body, outs, args, specs=None, scratch=(), flops=1 << 20, limit=32 << 20):
    outs = [jax.ShapeDtypeStruct(s, d) for s, d in outs]
    return pl.pallas_call(
        body,
        out_shape=outs,
        in_specs=specs or [VMEM] * len(args),
        out_specs=[VMEM] * len(outs),
        scratch_shapes=list(scratch),
        compiler_params=pltpu.CompilerParams(vmem_limit_bytes=limit),
        cost_estimate=pl.CostEstimate(flops=flops, bytes_accessed=4 << 20, transcendentals=0),
    )(*args)


def moved(shard, k):
    ny, nz, nx, nh, nc = (lax.axis_size(a) for a in AXES)

    def place(y, z, x, h, c):
        return (((y * nz + z) * nx + x) * nh + h) * nc + c

    pairs = []
    for y, z, x, h, c in itertools.product(*[range(n) for n in (ny, nz, nx, nh, nc)]):
        spot = (h * ny + y + turns(k, c)) % (ny * nh)
        other = (z, c) if z % 2 == c else (z ^ 1, 1 - c)
        pairs.append((place(spot % ny, other[0], x, spot // ny, other[1]), place(y, z, x, h, c)))
    return lax.ppermute(shard, AXES, pairs)


def turns(k, c):
    return (0, 1, -2 if c else 2, -1)[k]


def from_ring(shard, k):
    nh, ny = lax.axis_size("h"), lax.axis_size("y")
    ring = [y * nh + h for h in range(nh) for y in range(ny)]
    count = len(ring)
    pairs = [
        (ring[(i + turns(k, c)) % count] * 2 + c, ring[i] * 2 + c) for i in range(count) for c in range(2)
    ]
    return lax.ppermute(shard, ("y", "h", "c"), pairs)


def on_device(
    floor_tokens, token_table, depth_kernel, norm_gain, layer_scale, w_in, w_out, grad_out
):
    rows, cols = floor_tokens.shape
    chans = depth_kernel.shape[2]
    width = norm_gain.shape[0]
    blocks = width // chans
    copies = lax.axis_size("z") // 2
    hid = w_out.shape[0] * lax.axis_size("y")
    swap = [(0, 1), (1, 0)]

    (both,) = call(
        stack_kernel,
        [((2, *w_out.shape), BF16)],
        (w_in, w_out),
        [ANY] * 2,
        [pltpu.VMEM(w_in.shape, BF16), pltpu.SemaphoreType.DMA((2,))],
        limit=60 << 20,
    )
    near, far = moved(both, 0), moved(both, 2)
    low, high = edges(floor_tokens[:3] + 1, floor_tokens[rows - 3 :] + 1)
    taps = depth_kernel.reshape(49, chans).T
    scale = lax.dynamic_slice_in_dim(layer_scale, lax.axis_index(CHAN) * chans, chans, 0)[:, None]
    gain = jnp.broadcast_to(norm_gain[:, None], (width, cols))
    grad_local = grad_out.transpose(0, 2, 1)

    tile = (rows, chans, cols)
    packed = (blocks, 2, chans, cols)
    x_local, send = call(
        functools.partial(first_kernel, copies),
        [(tile, BF16), (packed, BF16)],
        (floor_tokens, low, high, token_table.T, taps, scale, grad_local),
    )
    weights = [from_ring(near, 1), from_ring(near, 3)]
    own = lax.all_to_all(send, CHAN, 0, 0, tiled=True)
    (anchor,) = call(anchor_kernel, [((16, 128), BF16)], (near, far), flops=20 << 30)
    own, anchor = lax.optimization_barrier((own, anchor))
    weights += [near, far, anchor]
    oth = lax.ppermute(own, "c", swap)
    keep, sib = call(
        middle_kernel,
        [(packed, F32), (packed, BF16)],
        (own, oth, gain, *weights),
        [VMEM] * 3 + [ANY] * 5,
        [
            pltpu.VMEM((hid, width), BF16),
            pltpu.VMEM((hid, width), BF16),
            pltpu.VMEM((width, 2 * cols), BF16),
            pltpu.VMEM((width, 2 * cols), BF16),
            pltpu.VMEM((width, 2 * cols), F32),
            pltpu.VMEM((width, 2 * cols), F32),
            pltpu.VMEM((hid, 2 * cols), BF16),
            pltpu.VMEM((hid, 2 * cols), BF16),
            pltpu.SemaphoreType.DMA((8,)),
        ],
        flops=8 * hid * width * 2 * cols,
        limit=40 << 20,
    )
    part = (keep + lax.ppermute(sib, "c", swap).astype(F32)).astype(BF16)
    got = lax.all_to_all(part, CHAN, 0, 0, tiled=True)
    edge = (3, chans, cols)
    block_out, gconv, low_side, high_side = call(
        functools.partial(sum_kernel, copies),
        [(tile, BF16), (tile, BF16), (edge, BF16), (edge, BF16)],
        (got, x_local, scale),
    )
    low, high = edges(low_side, high_side)
    (grad_embedded,) = call(last_kernel, [(tile, BF16)], (gconv, low, high, taps, grad_local))
    return block_out.transpose(0, 2, 1), grad_embedded.transpose(0, 2, 1)


def solution(mesh):
    chan, space = mesh.shape["chan"], mesh.shape["space"]
    grid = Mesh(mesh.devices.reshape(4, chan // 4, space // 4, 2, 2), AXES)
    placed = (
        P(SPACE, None),
        P(None, CHAN),
        P(None, None, CHAN),
        P(),
        P(),
        P(None, CHAN),
        P(CHAN, None),
        P(SPACE, None, CHAN),
    )
    return jax.shard_map(
        on_device,
        mesh=grid,
        in_specs=placed,
        out_specs=(P(SPACE, None, CHAN), P(SPACE, None, CHAN)),
        check_vma=False,
    )
```
